128 devices in a mesh: dp: 4 (over y), graph: 32 (over z, x, core).
Axes of the slice: x: 4, y: 4, z: 4, core: 2. Of those that a mesh axis runs over, the one named last changes fastest.
Arguments:
- edge_emb: bfloat16 [4, 16384, 512], P('dp', 'graph'), may hold values from -6 to 6
- atom_emb: bfloat16 [4, 1024, 512], P('dp', 'graph'), may hold values from -6 to 6
- edge_target: int32 [4, 16384], P('dp', 'graph'), may hold values from 0 to 1023, as said below
- trip_in: int32 [4, 524288], P('dp', 'graph'), may hold values from 0 to 16383, as said below
- trip_out: int32 [4, 524288], P('dp', 'graph'), may hold values from 0 to 511
- trip_count: int32 [4, 32], P('dp', 'graph'), may hold values from 8192 to 16384, as said below
- trip_basis: bfloat16 [4, 16, 524288], P('dp', None, 'graph'), may hold values from -3 to 3
- grad_edge: bfloat16 [4, 16384, 512], P('dp', 'graph'), may hold values from -6 to 6
- grad_atom: bfloat16 [4, 1024, 512], P('dp', 'graph'), may hold values from -6 to 6
- w_down: bfloat16 [512, 64], replicated, may hold values from -0.25 to 0.25
- w_bil: bfloat16 [1024, 64], replicated, may hold values from -0.1875 to 0.1875
- w_up: bfloat16 [64, 512], replicated, may hold values from -0.75 to 0.75
- w_atom: bfloat16 [512, 512], replicated, may hold values from -0.25 to 0.25
Outputs:
- edge_new: bfloat16 [4, 16384, 512], P('dp', 'graph')
- atom_new: bfloat16 [4, 1024, 512], P('dp', 'graph')
- grad_edge_in: float32 [4, 16384, 512], P('dp', 'graph')
- grad_wdown: float32 [512, 64], replicated
- grad_wbil: float32 [1024, 64], replicated
- grad_wup: float32 [64, 512], replicated
- grad_watom: float32 [512, 512], replicated
The draws below stay inside these ranges and needn't reach their ends.
Inputs may be any that keep to these rules, and one draw needn't show every extreme that they name: `trip_in`: among the 16384 slots of one device, the incoming edges held by any one device of the batch number at most 128 distinct ones; on every device some one device gives exactly 128. `trip_count`: every batch has a device with all 16384 slots used. `edge_target`: among the 512 edges of one device, those whose target atom is held by any one device (target // 32) number at most 32; on every device some one holder gets exactly 32.
All inputs are finite; a program needn't handle non-finite values.
Results may differ from the reference program's by a relative error of at most 0.0077.
Values may be sent and summed in bfloat16 or wider, within the bound.
A program may use at most 64 MiB of HBM per device.

```python
import math
import jax
import jax.numpy as jnp
from jax import lax

D = 512
DT = 64
NB = 16
EDGE_DEV = 512
ATOM_DEV = 32
TRIP_DEV = 16384
CAP = 128
GROUPS = 4
GROUP = 32
ACAP = 32
EDGES_G = 16384
ATOMS_G = 1024
TRIPLETS_G = 524288


def triplet_plan(key):
    base = jax.random.fold_in(key, 4242)
    subkeys = jax.random.split(base, 7)
    members = jnp.arange(GROUP, dtype=jnp.int32)
    counts = jax.random.randint(subkeys[0], (GROUPS, GROUP), TRIP_DEV // 2, TRIP_DEV + 1)
    fullest = jax.random.randint(subkeys[1], (GROUPS, 1), 0, GROUP)
    counts = jnp.where(members[None, :] == fullest, TRIP_DEV, counts)
    demand = jax.random.randint(subkeys[2], (GROUPS, GROUP, GROUP), 1, CAP + 1)
    busiest = jax.random.randint(subkeys[3], (GROUPS, GROUP, 1), 0, GROUP)
    demand = jnp.where(members[None, None, :] == busiest, CAP, demand)
    shuffles = jax.vmap(lambda subkey: jax.random.permutation(subkey, EDGE_DEV))(jax.random.split(subkeys[4], GROUPS * GROUP * GROUP))
    shuffles = shuffles.reshape(GROUPS, GROUP, GROUP, EDGE_DEV).astype(jnp.int32)
    bounds_end = jnp.cumsum(demand, axis=2)
    starts = bounds_end - demand
    totals = bounds_end[:, :, -1:]
    slot_ids = jnp.arange(TRIP_DEV, dtype=jnp.int32)[None, None, :]
    spare_pick = jax.random.randint(subkeys[5], (GROUPS, GROUP, TRIP_DEV), 0, 1 << 30) % totals
    wanted = jnp.where(slot_ids < totals, slot_ids, spare_pick)
    source = jax.vmap(lambda limits, picks: jnp.searchsorted(limits, picks, side='right'))(bounds_end.reshape(GROUPS * GROUP, GROUP), wanted.reshape(GROUPS * GROUP, TRIP_DEV))
    source = source.reshape(GROUPS, GROUP, TRIP_DEV).astype(jnp.int32)
    offsets = wanted - jnp.take_along_axis(starts, source, axis=2)
    group_axis = jnp.arange(GROUPS, dtype=jnp.int32)[:, None, None]
    device_axis = jnp.arange(GROUP, dtype=jnp.int32)[None, :, None]
    row_ids = shuffles[group_axis, device_axis, source, offsets]
    edge_ids = source * EDGE_DEV + row_ids
    scores = jax.random.randint(subkeys[6], (GROUPS, GROUP, TRIP_DEV), 0, TRIP_DEV)
    sort_key = jnp.where(slot_ids < counts[:, :, None], scores, TRIP_DEV + slot_ids)
    shuffle = jnp.argsort(sort_key, axis=2, stable=True)
    edge_ids = jnp.take_along_axis(edge_ids, shuffle, axis=2)
    return (edge_ids.reshape(GROUPS, GROUP * TRIP_DEV).astype(jnp.int32), counts.astype(jnp.int32))


def draw_trip_in(key, part):
    return triplet_plan(key)[0]


def draw_trip_count(key, part):
    return triplet_plan(key)[1]


def draw_edge_target(key, part):
    base = jax.random.fold_in(key, 7171)
    subkeys = jax.random.split(base, 4)
    lower = (EDGE_DEV + GROUP - 1) // GROUP
    demand = jax.random.randint(subkeys[0], (GROUPS, GROUP, GROUP), lower, ACAP + 1)
    demand = demand.at[:, :, 0].set(ACAP)
    ends = jnp.cumsum(demand, axis=2)
    slot_ids = jnp.arange(EDGE_DEV, dtype=jnp.int32)
    order_pos = jnp.sum((slot_ids[None, None, :, None] >= ends[:, :, None, :]).astype(jnp.int32), axis=3)
    first_owner = jax.random.randint(subkeys[1], (GROUPS, GROUP, 1), 0, GROUP)
    owner = (first_owner + order_pos) % GROUP
    local_atom = jax.random.randint(subkeys[2], (GROUPS, GROUP, EDGE_DEV), 0, ATOM_DEV)
    targets = owner * ATOM_DEV + local_atom
    shuffles = jax.vmap(lambda subkey: jax.random.permutation(subkey, EDGE_DEV))(jax.random.split(subkeys[3], GROUPS * GROUP)).reshape(GROUPS, GROUP, EDGE_DEV).astype(jnp.int32)
    targets = jnp.take_along_axis(targets, shuffles, axis=2)
    return targets.reshape(GROUPS, GROUP * EDGE_DEV).astype(jnp.int32)


def set_ends(entries, stream_key, least, top_value):
    longest = entries.shape.index(max(entries.shape))
    spots = []
    for shift in (0, 1):
        where = [jax.random.randint(jax.random.fold_in(stream_key, axis), (), 0, length) for axis, length in enumerate(entries.shape)]
        where[longest] = (where[longest] + shift) % entries.shape[longest]
        spots.append(tuple(where))
    return entries.at[spots[0]].set(least).at[spots[1]].set(top_value)


def shard_levels(key, extent, shards, smallest, high):
    factor_of, own = 1.0, jax.random.fold_in(key, 6)
    for axis_at, blocks in shards:
        draws = jnp.exp(jax.random.uniform(jax.random.fold_in(own, axis_at), (blocks,), jnp.float32, smallest / len(shards), high / len(shards)))
        factor_of = factor_of * jnp.repeat(draws, extent[axis_at] // blocks).reshape([-1 if axis == axis_at else 1 for axis in range(len(extent))])
    return factor_of


def bell_draw(own_key, dims, scale, most, shards=(), kind=jnp.bfloat16):
    entries = jax.random.normal(own_key, dims, jnp.float32) * scale
    if len(shards) > 0:
        entries = shard_levels(own_key, dims, shards, -0.22, 0.18) * entries
    return jnp.clip(entries, min=-most, max=most).astype(kind)


def setup_inputs(seed: int = 0) -> dict:
    splits = jax.random.split(jax.random.key(seed), 14)
    edge_emb = bell_draw(splits[0], (GROUPS, EDGES_G, D), 1.0, 6.0, ((0, 4), (1, 32)))
    atom_emb = bell_draw(splits[1], (GROUPS, ATOMS_G, D), 1.0, 6.0, ((0, 4), (1, 32)))
    edge_target = draw_edge_target(jax.random.fold_in(splits[13], 71), 0)
    trip_in = draw_trip_in(jax.random.fold_in(splits[13], 71), 0)
    trip_out = set_ends(jax.random.randint(splits[4], (GROUPS, TRIPLETS_G), 0, EDGE_DEV), jax.random.fold_in(splits[4], 1), 0, EDGE_DEV - 1).astype(jnp.int32)
    trip_count = draw_trip_count(jax.random.fold_in(splits[13], 71), 0)
    trip_basis = bell_draw(splits[6], (GROUPS, NB, TRIPLETS_G), 0.5, 3.0, ((0, 4), (2, 32)))
    grad_edge = bell_draw(splits[7], (GROUPS, EDGES_G, D), 1.0, 6.0, ((0, 4), (1, 32)))
    grad_atom = bell_draw(splits[8], (GROUPS, ATOMS_G, D), 1.0, 6.0, ((0, 4), (1, 32)))
    w_down = bell_draw(splits[9], (D, DT), D ** -0.5, 0.25)
    w_bil = bell_draw(splits[10], (NB * DT, DT), (NB * DT) ** -0.5, 0.1875)
    w_up = bell_draw(splits[11], (DT, D), DT ** -0.5, 0.75)
    w_atom = bell_draw(splits[12], (D, D), D ** -0.5, 0.25)
    return dict(edge_emb=edge_emb, atom_emb=atom_emb, edge_target=edge_target, trip_in=trip_in, trip_out=trip_out, trip_count=trip_count, trip_basis=trip_basis, grad_edge=grad_edge, grad_atom=grad_atom, w_down=w_down, w_bil=w_bil, w_up=w_up, w_atom=w_atom)


ATOM_SCALE = 0.25

def silu_slope(value):
    logistic = jax.nn.sigmoid(value)
    return logistic * (1.0 + value * (1.0 - logistic))

def spread_rows(basis_rows, feat_rows):
    outer = basis_rows.astype(jnp.float32)[:, :, None] * feat_rows.astype(jnp.float32)[:, None, :]
    return outer.reshape(basis_rows.shape[0], -1).astype(jnp.bfloat16)

def one_group(edge_emb, atom_emb, edge_target, trip_in, trip_out, trip_count, trip_basis, grad_edge, grad_atom, w_down, w_bil, w_up, w_atom):
    projected = jnp.dot(edge_emb, w_down, preferred_element_type=jnp.float32)
    edge_feat = jax.nn.silu(projected).astype(jnp.bfloat16)
    slot_ids = jnp.arange(TRIPLETS_G, dtype=jnp.int32)
    device = (slot_ids // TRIP_DEV).astype(jnp.int32)
    usable = slot_ids % TRIP_DEV < trip_count[device]
    out_edge = (device * EDGE_DEV + trip_out).astype(jnp.int32)
    feat_in = edge_feat[trip_in]
    basis_rows = trip_basis.T
    block_rows = math.gcd(TRIPLETS_G, 8192)
    feat_blocks = feat_in.reshape(-1, block_rows, DT)
    basis_blocks = basis_rows.reshape(-1, block_rows, NB)

    def forward_block(pair):
        return jnp.dot(spread_rows(pair[0], pair[1]), w_bil, preferred_element_type=jnp.float32)
    mixed = lax.map(forward_block, (basis_blocks, feat_blocks)).reshape(TRIPLETS_G, DT)
    mixed = jnp.where(usable[:, None], mixed, jnp.zeros((), jnp.float32))
    gathered = jax.ops.segment_sum(mixed, out_edge, num_segments=EDGES_G).astype(jnp.bfloat16)
    update = jnp.dot(gathered, w_up, preferred_element_type=jnp.float32)
    edge_new = (edge_emb.astype(jnp.float32) + jax.nn.silu(update)).astype(jnp.bfloat16)
    atom_sum = jax.ops.segment_sum(edge_new.astype(jnp.float32), edge_target, num_segments=ATOMS_G).astype(jnp.bfloat16)
    atom_pre = ATOM_SCALE * jnp.dot(atom_sum, w_atom, preferred_element_type=jnp.float32)
    atom_new = (atom_emb.astype(jnp.float32) + jax.nn.silu(atom_pre)).astype(jnp.bfloat16)
    grad_pre = (grad_atom.astype(jnp.float32) * silu_slope(atom_pre)).astype(jnp.bfloat16)
    watom_term = ATOM_SCALE * jnp.dot(atom_sum.T, grad_pre, preferred_element_type=jnp.float32)
    grad_sum = (ATOM_SCALE * jnp.dot(grad_pre, w_atom.T, preferred_element_type=jnp.float32)).astype(jnp.bfloat16)
    grad_new = grad_edge.astype(jnp.float32) + grad_sum[edge_target].astype(jnp.float32)
    grad_update = (grad_new * silu_slope(update)).astype(jnp.bfloat16)
    wup_term = jnp.dot(gathered.T, grad_update, preferred_element_type=jnp.float32)
    grad_gathered = jnp.dot(grad_update, w_up.T, preferred_element_type=jnp.float32).astype(jnp.bfloat16)
    grad_mixed = jnp.where(usable[:, None], grad_gathered[out_edge], jnp.zeros((), jnp.bfloat16))

    def backward_block(running, triple):
        basis_part, feat_part, grad_part = triple
        spread = spread_rows(basis_part, feat_part)
        running = running + jnp.dot(spread.T, grad_part, preferred_element_type=jnp.float32)
        backed = jnp.dot(grad_part, w_bil.T, preferred_element_type=jnp.float32).reshape(-1, NB, DT)
        feat_grad = lax.optimization_barrier(jnp.sum(basis_part.astype(jnp.float32)[:, :, None] * backed, axis=1))
        return (running, feat_grad)
    wbil_term, grad_feat = lax.scan(backward_block, jnp.zeros((NB * DT, DT), jnp.float32), (basis_blocks, feat_blocks, grad_mixed.reshape(-1, block_rows, DT)))
    grad_feat = grad_feat.reshape(TRIPLETS_G, DT)
    grad_edge_feat = jax.ops.segment_sum(grad_feat, trip_in, num_segments=EDGES_G)
    grad_project = (grad_edge_feat * silu_slope(projected)).astype(jnp.bfloat16)
    grad_edge_in = grad_new + jnp.dot(grad_project, w_down.T, preferred_element_type=jnp.float32)
    wdown_term = jnp.dot(edge_emb.T, grad_project, preferred_element_type=jnp.float32)
    return (edge_new, atom_new, grad_edge_in, wdown_term, wbil_term, wup_term, watom_term)

def reference(edge_emb, atom_emb, edge_target, trip_in, trip_out, trip_count, trip_basis, grad_edge, grad_atom, w_down, w_bil, w_up, w_atom):
    edge_list = []
    atom_list = []
    input_list = []
    sums = None
    for group in range(GROUPS):
        result = one_group(edge_emb[group], atom_emb[group], edge_target[group], trip_in[group], trip_out[group], trip_count[group], trip_basis[group], grad_edge[group], grad_atom[group], w_down, w_bil, w_up, w_atom)
        edge_list.append(result[0])
        atom_list.append(result[1])
        input_list.append(result[2])
        terms = result[3:]
        sums = terms if sums is None else tuple((left + right for left, right in zip(sums, terms)))
    factor = 1.0 / math.sqrt(GROUPS * EDGES_G)
    return (jnp.stack(edge_list), jnp.stack(atom_list), jnp.stack(input_list), sums[0] * factor, sums[1] * factor, sums[2] * factor, sums[3] * factor)
```

```python
import functools
import math

import jax
import jax.numpy as jnp
from jax import lax
from jax.experimental import pallas as pl
from jax.experimental.pallas import tpu as pltpu
from jax.sharding import PartitionSpec as P

MESH = pl.DeviceIdType.MESH
F32 = jnp.float32
BF16 = jnp.bfloat16
ATOM_SCALE = 0.25
CAP = 128
LANES = 128
NEAR = 4
BLOCK = 1024
ANY = pl.BlockSpec(memory_space=pl.ANY)
VMEM = pl.BlockSpec(memory_space=pltpu.VMEM)
NN = (((1,), (0,)), ((), ()))
NT = (((1,), (1,)), ((), ()))
TN = (((0,), (0,)), ((), ()))


def dot(a, b, dims=NN):
    return lax.dot_general(a, b, dims, preferred_element_type=F32)


def two_part_dot(a, b, dims=NN):
    high = a.astype(BF16)
    low = (a - high.astype(F32)).astype(BF16)
    return dot(high, b, dims) + dot(low, b, dims)


def rows_of(shape):
    return lax.broadcasted_iota(jnp.int32, shape, 0)


def hot(index, size):
    return (rows_of((size, index.shape[1])) == index).astype(F32).astype(BF16)


def silu_slope(value):
    logistic = jax.nn.sigmoid(value)
    return logistic * (1.0 + value * (1.0 - logistic))


def silu(value):
    return value * jax.nn.sigmoid(value)


def params(**kw):
    return pltpu.CompilerParams(vmem_limit_bytes=60 * 1024 * 1024, **kw)


def exchange_kernel(peers, source_at, target_at, x_ref, o_ref, send, recv, own):
    me = lax.axis_index("graph")
    barrier = pltpu.get_barrier_semaphore()

    def greet(k, c):
        pl.semaphore_signal(
            barrier, inc=1, device_id={"graph": lax.rem(me + k, peers)}, device_id_type=MESH
        )
        return c

    lax.fori_loop(1, peers, greet, 0)
    mine = pltpu.make_async_copy(source_at(x_ref, me), target_at(o_ref, me), own)
    mine.start()
    pl.semaphore_wait(barrier, peers - 1)

    def copy(k):
        peer = lax.rem(me + k, peers)
        return pltpu.make_async_remote_copy(
            src_ref=source_at(x_ref, peer),
            dst_ref=target_at(o_ref, me),
            send_sem=send.at[k],
            recv_sem=recv.at[k],
            device_id={"graph": peer},
            device_id_type=MESH,
        )

    def start(k, c):
        copy(k).start()
        return c

    def finish(k, c):
        copy(k).wait()
        return c

    lax.fori_loop(1, peers, start, 0)
    mine.wait()
    lax.fori_loop(1, peers, finish, 0)


def exchange(value, out_shape, source_at, target_at, peers, key):
    return pl.pallas_call(
        functools.partial(exchange_kernel, peers, source_at, target_at),
        out_shape=jax.ShapeDtypeStruct(out_shape, value.dtype),
        in_specs=[ANY],
        out_specs=ANY,
        scratch_shapes=[
            pltpu.SemaphoreType.DMA((peers,)),
            pltpu.SemaphoreType.DMA((peers,)),
            pltpu.SemaphoreType.DMA,
        ],
        compiler_params=params(collective_id=key, has_side_effects=True),
        name=f"exchange_{key}",
    )(value)


def whole_block(ref, index):
    return ref


def lead_block(ref, index):
    return ref.at[index]


def tile_block(ref, index):
    width = ref.shape[1] // NEAR
    rows = 64
    return ref.at[
        pl.ds(pl.multiple_of(lax.div(index, NEAR) * rows, rows), rows),
        pl.ds(pl.multiple_of(lax.rem(index, NEAR) * width, width), width),
    ]


def lane_block(ref, index):
    return ref.at[:, pl.ds(pl.multiple_of(index * CAP, CAP), CAP)]


def row_block(rows, ref, index):
    return ref.at[pl.ds(pl.multiple_of(index * rows, rows), rows), :]


def names_kernel(blocks, members, in_ref, emb_ref, wdt_ref, rank_ref, slot_ref, proj_ref, feat_ref, table, found):
    step = pl.program_id(0)
    highs = table.shape[0]
    per = highs // members
    index = in_ref[...]
    high = lax.shift_right_logical(index, 7)
    low = lax.bitwise_and(index, LANES - 1)

    @pl.when(step == 0)
    def _():
        found[...] = jnp.zeros_like(found)
        proj = dot(wdt_ref[...], emb_ref[...], NT)
        proj_ref[...] = proj
        feat_ref[...] = silu(proj).astype(BF16)

    @pl.when(step < blocks)
    def _():
        found[...] += dot(hot(high, highs), hot(low, LANES), NT)

    @pl.when(step == blocks - 1)
    def _():
        there = jnp.where(found[...] > 0.0, 1.0, 0.0)
        there16 = there.astype(BF16)
        row = lax.broadcasted_iota(jnp.int32, (LANES, LANES), 0)
        col = lax.broadcasted_iota(jnp.int32, (LANES, LANES), 1)
        upper = (row <= col).astype(F32).astype(BF16)
        hrow = lax.broadcasted_iota(jnp.int32, (highs, highs), 0)
        hcol = lax.broadcasted_iota(jnp.int32, (highs, highs), 1)
        before = ((hcol < hrow) & (lax.div(hcol, per) == lax.div(hrow, per))).astype(F32).astype(BF16)
        ahead = dot(before, there16).astype(BF16)
        ones = jnp.ones((LANES, LANES), BF16)
        rank = dot(there16, upper) + dot(ahead, ones) - 1.0
        rank = jnp.where(there > 0.0, rank, -1.0)
        table[...] = rank.astype(BF16)
        for s in range(members):
            rank_ref[s] = rank[s * per : (s + 1) * per, :]

    @pl.when(step >= blocks)
    def _():
        ranks = dot(table[...], hot(high, highs), TN)
        picked = jnp.where(rows_of(ranks.shape) == low, ranks, 0.0)
        rank = jnp.sum(picked, axis=0, keepdims=True).astype(jnp.int32)
        near = lax.bitwise_and(lax.div(high, per), NEAR - 1)
        slot_ref[...] = near * CAP + rank


def names(incoming, emb, wdt, members):
    slots = incoming.shape[1]
    edges = emb.shape[0]
    width = wdt.shape[0]
    block = math.gcd(slots, 2 * BLOCK)
    blocks = slots // block
    highs = members * edges // LANES
    per = highs // members
    return pl.pallas_call(
        functools.partial(names_kernel, blocks, members),
        grid=(2 * blocks,),
        out_shape=(
            jax.ShapeDtypeStruct((members, per, LANES), F32),
            jax.ShapeDtypeStruct((1, slots), jnp.int32),
            jax.ShapeDtypeStruct((width, edges), F32),
            jax.ShapeDtypeStruct((width, edges), BF16),
        ),
        in_specs=[
            pl.BlockSpec((1, block), lambda i: (0, lax.rem(i, blocks))),
            pl.BlockSpec(emb.shape, lambda i: (0, 0)),
            pl.BlockSpec(wdt.shape, lambda i: (0, 0)),
        ],
        out_specs=(
            pl.BlockSpec((members, per, LANES), lambda i: (0, 0, 0)),
            pl.BlockSpec((1, block), lambda i: (0, lax.max(i - blocks, 0))),
            pl.BlockSpec((width, edges), lambda i: (0, 0)),
            pl.BlockSpec((width, edges), lambda i: (0, 0)),
        ),
        scratch_shapes=[pltpu.VMEM((highs, LANES), BF16), pltpu.VMEM((highs, LANES), F32)],
        compiler_params=params(),
        name="names",
    )(incoming, emb, wdt)


def chosen_hot(rank_ref, member):
    per = rank_ref.shape[1]
    ranks = rank_ref[member]
    place = lax.broadcasted_iota(jnp.int32, (CAP, LANES), 0).astype(F32)
    return jnp.concatenate(
        [(place == ranks[q : q + 1, :]).astype(F32).astype(BF16) for q in range(per)], axis=1
    )


def select_kernel(members, rank_ref, feat_ref, out_ref):
    def one(d, c):
        out_ref[d] = dot(feat_ref[...], chosen_hot(rank_ref, d), NT).astype(BF16)
        return c

    lax.fori_loop(0, members, one, 0)


def select(ranks, feat):
    members = ranks.shape[0]
    return pl.pallas_call(
        functools.partial(select_kernel, members),
        out_shape=jax.ShapeDtypeStruct((members, feat.shape[0], CAP), BF16),
        in_specs=[VMEM, VMEM],
        out_specs=VMEM,
        compiler_params=params(),
        name="select",
    )(ranks, feat)


def forward_kernel(
    blocks, edges, far, table_ref, slot_ref, in_ref, out_ref, count_ref, basis_ref, total_ref, spread
):
    step = pl.program_id(0)
    block = slot_ref.shape[1]
    width = table_ref.shape[0] // far
    shift = edges.bit_length() - 1 + NEAR.bit_length() - 1

    @pl.when(step == 0)
    def _():
        total_ref[...] = jnp.zeros_like(total_ref)

    group = lax.shift_right_logical(in_ref[...], shift)
    wide = dot(table_ref[...], hot(slot_ref[...], table_ref.shape[1]))
    feat = wide[0:width]
    for k in range(1, far):
        feat = jnp.where(group == k, wide[k * width : (k + 1) * width], feat)
    basis = basis_ref[...].astype(F32)
    for b in range(basis.shape[0]):
        spread[b * width : (b + 1) * width, :] = (basis[b : b + 1, :] * feat).astype(BF16)
    at = step * block + lax.broadcasted_iota(jnp.int32, (1, block), 1)
    place = jnp.where(at < count_ref[0, 0], out_ref[...], -1)
    total_ref[...] += dot(spread[...], hot(place, edges), NT)


def forward(table, slots, incoming, outgoing, count, basis, edges):
    total = slots.shape[1]
    block = math.gcd(total, BLOCK)
    blocks = total // block
    far = table.shape[0] // 64
    rows = basis.shape[0] * 64
    line = pl.BlockSpec((1, block), lambda i: (0, i))
    return pl.pallas_call(
        functools.partial(forward_kernel, blocks, edges, far),
        grid=(blocks,),
        out_shape=jax.ShapeDtypeStruct((rows, edges), F32),
        in_specs=[
            pl.BlockSpec(table.shape, lambda i: (0, 0)),
            line,
            line,
            line,
            pl.BlockSpec(memory_space=pltpu.SMEM),
            pl.BlockSpec((basis.shape[0], block), lambda i: (0, i)),
        ],
        out_specs=pl.BlockSpec((rows, edges), lambda i: (0, 0)),
        scratch_shapes=[pltpu.VMEM((rows, block), BF16)],
        compiler_params=params(),
        name="forward",
    )(table, slots, incoming, outgoing, count, basis)


def edges_kernel(total_ref, wbt_ref, wup_ref, emb_ref, target_ref, gath_ref, new_ref, slope_ref, atoms_ref):
    total = total_ref[...]
    high = total.astype(BF16)
    low = (total - high.astype(F32)).astype(BF16)
    gathered = (dot(wbt_ref[...], high) + dot(wbt_ref[...], low)).astype(BF16)
    gath_ref[...] = gathered
    update = dot(gathered, wup_ref[...], TN)
    new = (emb_ref[...].astype(F32) + silu(update)).astype(BF16)
    new_ref[...] = new
    slope_ref[...] = silu_slope(update)
    atoms_ref[...] = dot(hot(target_ref[...], atoms_ref.shape[0]), new).astype(BF16)


def edges_forward(total, wbt, wup, emb, targets, atoms):
    edges, wide = emb.shape
    return pl.pallas_call(
        edges_kernel,
        out_shape=(
            jax.ShapeDtypeStruct((wbt.shape[0], edges), BF16),
            jax.ShapeDtypeStruct((edges, wide), BF16),
            jax.ShapeDtypeStruct((edges, wide), F32),
            jax.ShapeDtypeStruct((atoms, wide), BF16),
        ),
        in_specs=[VMEM] * 5,
        out_specs=(VMEM,) * 4,
        compiler_params=params(),
        name="edges",
    )(total, wbt, wup, emb, targets)


def atoms_kernel(part_ref, watom_ref, emb_ref, grad_ref, new_ref, term_ref, sum_ref):
    total = jnp.sum(part_ref[...].astype(F32), axis=0).astype(BF16)
    pre = ATOM_SCALE * dot(total, watom_ref[...])
    new_ref[...] = (emb_ref[...].astype(F32) + silu(pre)).astype(BF16)
    grad_pre = (grad_ref[...].astype(F32) * silu_slope(pre)).astype(BF16)
    term_ref[...] = ATOM_SCALE * dot(total, grad_pre, TN)
    sum_ref[...] = (ATOM_SCALE * dot(grad_pre, watom_ref[...], NT)).astype(BF16)


def atoms_step(parts, watom, emb, grad):
    return pl.pallas_call(
        atoms_kernel,
        out_shape=(
            jax.ShapeDtypeStruct(emb.shape, BF16),
            jax.ShapeDtypeStruct(watom.shape, F32),
            jax.ShapeDtypeStruct(emb.shape, BF16),
        ),
        in_specs=[VMEM] * 4,
        out_specs=(VMEM,) * 3,
        compiler_params=params(),
        name="atoms",
    )(parts, watom, emb, grad)


def turn_kernel(all_ref, target_ref, grad_ref, slope_ref, wup_ref, gath_ref, total_ref, new_ref, up_ref, bil_ref, gg_ref):
    picked = dot(hot(target_ref[...], all_ref.shape[0]), all_ref[...], TN)
    new = grad_ref[...].astype(F32) + picked
    new_ref[...] = new
    update = (new * slope_ref[...]).astype(BF16)
    up_ref[...] = dot(gath_ref[...], update)
    gg = dot(wup_ref[...], update, NT).astype(BF16)
    gg_ref[...] = gg
    total = total_ref[...]
    high = total.astype(BF16)
    low = (total - high.astype(F32)).astype(BF16)
    bil_ref[...] = dot(gg, high, NT) + dot(gg, low, NT)


def turn(grad_all, targets, grad_edge, slope, wup, gathered, total):
    return pl.pallas_call(
        turn_kernel,
        out_shape=(
            jax.ShapeDtypeStruct(grad_edge.shape, F32),
            jax.ShapeDtypeStruct(wup.shape, F32),
            jax.ShapeDtypeStruct((wup.shape[0], total.shape[0]), F32),
            jax.ShapeDtypeStruct(gathered.shape, BF16),
        ),
        in_specs=[VMEM] * 7,
        out_specs=(VMEM,) * 4,
        compiler_params=params(),
        name="turn",
    )(grad_all, targets, grad_edge, slope, wup, gathered, total)


def backward_kernel(
    blocks, edges, far, gg_ref, slot_ref, in_ref, out_ref, count_ref, basis_ref, wbil_ref, sent_ref, total, spread
):
    step = pl.program_id(0)
    block = slot_ref.shape[1]
    width = gg_ref.shape[0]
    shift = edges.bit_length() - 1 + NEAR.bit_length() - 1

    @pl.when(step == 0)
    def _():
        total[...] = jnp.zeros_like(total)

    at = step * block + lax.broadcasted_iota(jnp.int32, (1, block), 1)
    place = jnp.where(at < count_ref[0, 0], out_ref[...], -1)
    picked = dot(gg_ref[...], hot(place, edges)).astype(BF16)
    backed = dot(wbil_ref[...], picked)
    basis = basis_ref[...].astype(F32)
    grad = basis[0:1, :] * backed[0:width]
    for b in range(1, basis.shape[0]):
        grad = grad + basis[b : b + 1, :] * backed[b * width : (b + 1) * width]
    group = lax.shift_right_logical(in_ref[...], shift)
    for k in range(far):
        spread[k * width : (k + 1) * width, :] = jnp.where(group == k, grad, 0.0).astype(BF16)
    total[...] += dot(spread[...], hot(slot_ref[...], total.shape[1]), NT)

    @pl.when(step == blocks - 1)
    def _():
        sent_ref[...] = total[...].astype(BF16)


def backward(gg, slots, incoming, outgoing, count, basis, wbil, far):
    width, edges = gg.shape
    total = slots.shape[1]
    block = math.gcd(total, BLOCK)
    blocks = total // block
    line = pl.BlockSpec((1, block), lambda i: (0, i))
    shape = (far * width, NEAR * CAP)
    return pl.pallas_call(
        functools.partial(backward_kernel, blocks, edges, far),
        grid=(blocks,),
        out_shape=jax.ShapeDtypeStruct(shape, BF16),
        in_specs=[
            pl.BlockSpec(gg.shape, lambda i: (0, 0)),
            line,
            line,
            line,
            pl.BlockSpec(memory_space=pltpu.SMEM),
            pl.BlockSpec((basis.shape[0], block), lambda i: (0, i)),
            pl.BlockSpec(wbil.shape, lambda i: (0, 0)),
        ],
        out_specs=pl.BlockSpec(shape, lambda i: (0, 0)),
        scratch_shapes=[pltpu.VMEM(shape, F32), pltpu.VMEM((far * width, block), BF16)],
        compiler_params=params(),
        name="backward",
    )(gg, slots, incoming, outgoing, count, basis, wbil)


def last_kernel(members, back_ref, rank_ref, proj_ref, wdt_ref, emb_ref, new_ref, in_ref, down_ref):
    def one(d, total):
        block = back_ref[:, pl.ds(pl.multiple_of(d * CAP, CAP), CAP)]
        return total + dot(block, chosen_hot(rank_ref, d))

    grad = lax.fori_loop(0, members, one, jnp.zeros(proj_ref.shape, F32))
    grad = (grad * silu_slope(proj_ref[...])).astype(BF16)
    in_ref[...] = new_ref[...] + dot(grad, wdt_ref[...], TN)
    down_ref[...] = dot(grad, emb_ref[...])


def last(back, ranks, proj, wdt, emb, grad_new):
    return pl.pallas_call(
        functools.partial(last_kernel, ranks.shape[0]),
        out_shape=(
            jax.ShapeDtypeStruct(grad_new.shape, F32),
            jax.ShapeDtypeStruct(wdt.shape, F32),
        ),
        in_specs=[VMEM] * 6,
        out_specs=(VMEM,) * 2,
        compiler_params=params(),
        name="last",
    )(back, ranks, proj, wdt, emb, grad_new)


def body(
    groups,
    members,
    edge_emb,
    atom_emb,
    edge_target,
    trip_in,
    trip_out,
    trip_count,
    trip_basis,
    grad_edge,
    grad_atom,
    w_down,
    w_bil,
    w_up,
    w_atom,
):
    emb = edge_emb[0]
    edges = emb.shape[0]
    atom_dev, wide = atom_emb.shape[1:]
    atoms = atom_dev * members
    far = members // NEAR
    wdt = w_down.T
    wbt = w_bil.T
    width = wdt.shape[0]
    basis = trip_basis[0]

    ranks, slots, proj, feat = names(trip_in, emb, wdt, members)
    wanted = exchange(ranks, ranks.shape, lead_block, lead_block, members, 1)
    chosen = select(wanted, feat)
    table = exchange(chosen, (far * width, NEAR * CAP), lead_block, tile_block, members, 2)
    total = forward(table, slots, trip_in, trip_out, trip_count, basis, edges)
    gathered, edge_new, slope, parts = edges_forward(total, wbt, w_up, emb, edge_target, atoms)
    parts = exchange(
        parts, (members, atom_dev, wide), functools.partial(row_block, atom_dev), lead_block, members, 3
    )
    atom_new, watom_term, grad_sum = atoms_step(parts, w_atom, atom_emb[0], grad_atom[0])
    grad_all = exchange(
        grad_sum, (atoms, wide), whole_block, functools.partial(row_block, atom_dev), members, 4
    )
    grad_new, wup_term, wbil_term, gg = turn(
        grad_all, edge_target, grad_edge[0], slope, w_up, gathered, total
    )
    sent = backward(gg, slots, trip_in, trip_out, trip_count, basis, w_bil, far)
    back = exchange(sent, (width, members * CAP), tile_block, lane_block, members, 5)
    grad_in, wdown_term = last(back, wanted, proj, wdt, emb, grad_new)
    down, bil, up, atom = lax.psum((wdown_term, wbil_term, wup_term, watom_term), ("dp", "graph"))
    factor = 1.0 / math.sqrt(groups * members * edges)
    return (
        edge_new[None],
        atom_new[None],
        grad_in[None],
        (down * factor).T,
        (bil * factor).T,
        up * factor,
        atom * factor,
    )


def solution(mesh):
    graph = P("dp", "graph")
    rows = P("dp", "graph", None)
    return jax.shard_map(
        functools.partial(body, mesh.shape["dp"], mesh.shape["graph"]),
        mesh=mesh,
        in_specs=(rows, rows, graph, graph, graph, graph, P("dp", None, "graph"), rows, rows)
        + (P(),) * 4,
        out_specs=(rows, rows, rows) + (P(),) * 4,
        check_vma=False,
    )
```

```python
import functools
import math

import jax
import jax.numpy as jnp
from jax import lax
from jax.experimental import pallas as pl
from jax.experimental.pallas import tpu as pltpu
from jax.sharding import PartitionSpec as P

MESH = pl.DeviceIdType.MESH
F32 = jnp.float32
BF16 = jnp.bfloat16
ATOM_SCALE = 0.25
CAP = 128
LANES = 128
NEAR = 4
BLOCK = 1024
ANY = pl.BlockSpec(memory_space=pl.ANY)
VMEM = pl.BlockSpec(memory_space=pltpu.VMEM)
NN = (((1,), (0,)), ((), ()))
NT = (((1,), (1,)), ((), ()))
TN = (((0,), (0,)), ((), ()))


def dot(a, b, dims=NN):
    return lax.dot_general(a, b, dims, preferred_element_type=F32)


def two_part_dot(a, b, dims=NN):
    high = a.astype(BF16)
    low = (a - high.astype(F32)).astype(BF16)
    return dot(high, b, dims) + dot(low, b, dims)


def rows_of(shape):
    return lax.broadcasted_iota(jnp.int32, shape, 0)


def hot(index, size):
    return (rows_of((size, index.shape[1])) == index).astype(F32).astype(BF16)


def silu_slope(value):
    logistic = jax.nn.sigmoid(value)
    return logistic * (1.0 + value * (1.0 - logistic))


def silu(value):
    return value * jax.nn.sigmoid(value)


def params(**kw):
    return pltpu.CompilerParams(vmem_limit_bytes=60 * 1024 * 1024, **kw)


def send_to(src, dst, send, recv, **where):
    return pltpu.make_async_remote_copy(
        src_ref=src,
        dst_ref=dst,
        send_sem=send,
        recv_sem=recv,
        device_id=where,
        device_id_type=MESH,
    )


def each(first, last, act):
    def one(k, c):
        act(k)
        return c

    lax.fori_loop(first, last, one, 0)


def some_rows(ref, index, rows):
    return ref.at[pl.ds(pl.multiple_of(index * rows, rows), rows), :]


def some_lanes(ref, index, lanes):
    return ref.at[:, pl.ds(pl.multiple_of(index * lanes, lanes), lanes)]


def tile_of(ref, row, rows, lane, lanes):
    return ref.at[
        pl.ds(pl.multiple_of(row * rows, rows), rows),
        pl.ds(pl.multiple_of(lane * lanes, lanes), lanes),
    ]


def greet(barrier, members, groups):
    me = lax.axis_index("graph")
    group = lax.axis_index("dp")
    each(
        1,
        members,
        lambda k: pl.semaphore_signal(
            barrier, inc=1, device_id={"graph": lax.rem(me + k, members)}, device_id_type=MESH
        ),
    )
    if groups > 1:
        each(
            1,
            groups,
            lambda k: pl.semaphore_signal(
                barrier, inc=1, device_id={"dp": lax.rem(group + k, groups)}, device_id_type=MESH
            ),
        )


def hot_of_ranks(rank_ref, hot_ref):
    members, per = rank_ref.shape[:2]
    place = lax.broadcasted_iota(jnp.int32, (CAP, LANES), 0).astype(F32)

    def one(d):
        ranks = rank_ref[d]
        at = pl.ds(pl.multiple_of(d * CAP, CAP), CAP)
        for q in range(per):
            hot_ref[at, q * LANES : (q + 1) * LANES] = (
                (place == ranks[q : q + 1, :]).astype(F32).astype(BF16)
            )

    each(0, members, one)


def early_kernel(
    members,
    far,
    in_ref,
    emb_ref,
    wdt_ref,
    wanted_ref,
    slot_ref,
    proj_ref,
    table_ref,
    table,
    found,
    rank_buf,
    hots,
    chosen,
    a_send,
    a_recv,
    b_send,
    b_recv,
):
    me = lax.axis_index("graph")
    barrier = pltpu.get_barrier_semaphore()
    greet(barrier, members, 1)
    highs = table.shape[0]
    per = highs // members
    width = wdt_ref.shape[0]
    block = math.gcd(in_ref.shape[1], 2 * BLOCK)
    blocks = in_ref.shape[1] // block

    def parts(i):
        index = in_ref[:, pl.ds(pl.multiple_of(i * block, block), block)]
        return lax.shift_right_logical(index, 7), lax.bitwise_and(index, LANES - 1)

    found[...] = jnp.zeros_like(found)

    def find(i):
        high, low = parts(i)
        found[...] += dot(hot(high, highs), hot(low, LANES), NT)

    each(0, blocks, find)
    there = jnp.where(found[...] > 0.0, 1.0, 0.0)
    there16 = there.astype(BF16)
    row = lax.broadcasted_iota(jnp.int32, (LANES, LANES), 0)
    col = lax.broadcasted_iota(jnp.int32, (LANES, LANES), 1)
    upper = (row <= col).astype(F32).astype(BF16)
    hrow = lax.broadcasted_iota(jnp.int32, (highs, highs), 0)
    hcol = lax.broadcasted_iota(jnp.int32, (highs, highs), 1)
    before = ((hcol < hrow) & (lax.div(hcol, per) == lax.div(hrow, per))).astype(F32).astype(BF16)
    ahead = dot(before, there16).astype(BF16)
    ones = jnp.ones((LANES, LANES), BF16)
    rank = dot(there16, upper) + dot(ahead, ones) - 1.0
    rank = jnp.where(there > 0.0, rank, -1.0)
    table[...] = rank.astype(BF16)
    for s in range(members):
        rank_buf[s] = rank[s * per : (s + 1) * per, :]
    proj = dot(wdt_ref[...], emb_ref[...], NT)
    proj_ref[...] = proj
    feat = silu(proj).astype(BF16)
    pl.semaphore_wait(barrier, members - 1)

    def rank_copy(k):
        peer = lax.rem(me + k, members)
        return send_to(rank_buf.at[peer], wanted_ref.at[me], a_send.at[k], a_recv.at[k], graph=peer)

    each(1, members, lambda k: rank_copy(k).start())
    wanted_ref[me] = rank_buf[me]

    def look(i):
        high, low = parts(i)
        ranks = dot(table[...], hot(high, highs), TN)
        picked = jnp.where(rows_of(ranks.shape) == low, ranks, 0.0)
        rank = jnp.sum(picked, axis=0, keepdims=True).astype(jnp.int32)
        near = lax.bitwise_and(lax.div(high, per), NEAR - 1)
        slot_ref[:, pl.ds(pl.multiple_of(i * block, block), block)] = near * CAP + rank

    each(0, blocks, look)
    each(1, members, lambda k: rank_copy(k).wait())
    hot_of_ranks(wanted_ref, hots)
    chosen[...] = dot(feat, hots[...], NT).astype(BF16)

    def place(ref, index):
        return tile_of(ref, lax.div(index, NEAR), width, lax.rem(index, NEAR), CAP)

    def feat_copy(k):
        peer = lax.rem(me + k, members)
        return send_to(
            some_lanes(chosen, peer, CAP), place(table_ref, me), b_send.at[k], b_recv.at[k], graph=peer
        )

    each(1, members, lambda k: feat_copy(k).start())
    place(table_ref, me)[...] = some_lanes(chosen, me, CAP)[...]
    each(1, members, lambda k: feat_copy(k).wait())


def early(incoming, emb, wdt, members):
    slots = incoming.shape[1]
    edges = emb.shape[0]
    width = wdt.shape[0]
    far = members // NEAR
    highs = members * edges // LANES
    per = highs // members
    return pl.pallas_call(
        functools.partial(early_kernel, members, far),
        out_shape=(
            jax.ShapeDtypeStruct((members, per, LANES), F32),
            jax.ShapeDtypeStruct((1, slots), jnp.int32),
            jax.ShapeDtypeStruct((width, edges), F32),
            jax.ShapeDtypeStruct((far * width, NEAR * CAP), BF16),
        ),
        in_specs=[VMEM] * 3,
        out_specs=(VMEM,) * 4,
        scratch_shapes=[
            pltpu.VMEM((highs, LANES), BF16),
            pltpu.VMEM((highs, LANES), F32),
            pltpu.VMEM((members, per, LANES), F32),
            pltpu.VMEM((members * CAP, edges), BF16),
            pltpu.VMEM((width, members * CAP), BF16),
        ]
        + [pltpu.SemaphoreType.DMA((members,))] * 4,
        compiler_params=params(collective_id=1, has_side_effects=True),
        name="early",
    )(incoming, emb, wdt)


def forward_kernel(
    blocks, edges, far, table_ref, slot_ref, in_ref, out_ref, count_ref, basis_ref, total_ref, spread
):
    step = pl.program_id(0)
    block = slot_ref.shape[1]
    width = table_ref.shape[0] // far
    shift = edges.bit_length() - 1 + NEAR.bit_length() - 1

    @pl.when(step == 0)
    def _():
        total_ref[...] = jnp.zeros_like(total_ref)

    group = lax.shift_right_logical(in_ref[...], shift)
    wide = dot(table_ref[...], hot(slot_ref[...], table_ref.shape[1]))
    feat = wide[0:width]
    for k in range(1, far):
        feat = jnp.where(group == k, wide[k * width : (k + 1) * width], feat)
    basis = basis_ref[...].astype(F32)
    for b in range(basis.shape[0]):
        spread[b * width : (b + 1) * width, :] = (basis[b : b + 1, :] * feat).astype(BF16)
    at = step * block + lax.broadcasted_iota(jnp.int32, (1, block), 1)
    place = jnp.where(at < count_ref[0, 0], out_ref[...], -1)
    total_ref[...] += dot(spread[...], hot(place, edges), NT)


def forward(table, slots, incoming, outgoing, count, basis, edges):
    total = slots.shape[1]
    block = math.gcd(total, BLOCK)
    blocks = total // block
    far = table.shape[0] // 64
    rows = basis.shape[0] * 64
    line = pl.BlockSpec((1, block), lambda i: (0, i))
    return pl.pallas_call(
        functools.partial(forward_kernel, blocks, edges, far),
        grid=(blocks,),
        out_shape=jax.ShapeDtypeStruct((rows, edges), F32),
        in_specs=[
            pl.BlockSpec(table.shape, lambda i: (0, 0)),
            line,
            line,
            line,
            pl.BlockSpec(memory_space=pltpu.SMEM),
            pl.BlockSpec((basis.shape[0], block), lambda i: (0, i)),
        ],
        out_specs=pl.BlockSpec((rows, edges), lambda i: (0, 0)),
        scratch_shapes=[pltpu.VMEM((rows, block), BF16)],
        compiler_params=params(),
        name="forward",
    )(table, slots, incoming, outgoing, count, basis)


def late_kernel(
    members,
    groups,
    far,
    scale,
    total_ref,
    wbt_ref,
    wup_ref,
    emb_ref,
    target_ref,
    watom_ref,
    atom_ref,
    gatom_ref,
    gedge_ref,
    slot_ref,
    in_ref,
    out_ref,
    count_ref,
    basis_ref,
    wbil_ref,
    wanted_ref,
    proj_ref,
    wdt_ref,
    new_ref,
    anew_ref,
    gin_ref,
    down_ref,
    bil_ref,
    up_ref,
    gat_ref,
    parts,
    half,
    pair,
    arrived,
    grads,
    slope,
    gnew,
    wa,
    wa_half,
    wa_pair,
    wa_in,
    wa_dp,
    wa_all,
    wb,
    wb_half,
    wb_pair,
    wb_in,
    wb_dp,
    wb_all,
    names,
    spread,
    sent,
    back,
    hots,
    wd,
    wd_in,
    wd_dp,
    wd_all,
    far_send,
    far_recv,
    duo_send,
    duo_recv,
    dp_send,
    dp_recv,
):
    me = lax.axis_index("graph")
    group = lax.axis_index("dp")
    chips = members // 2
    chip = lax.div(me, 2)
    core = lax.rem(me, 2)
    other = 1 - core
    partner = 2 * chip + other
    barrier = pltpu.get_barrier_semaphore()
    greet(barrier, members, groups)

    def chip_at(k):
        return lax.rem(chip + k, chips)

    def chip_from(k):
        return lax.rem(chip + chips - k, chips)

    def mine(c):
        return core * chips + c

    def theirs(c):
        return other * chips + c

    atom_dev, wide = atom_ref.shape
    edges = emb_ref.shape[0]
    width = wbt_ref.shape[0]
    total = total_ref[...]
    high = total.astype(BF16)
    low = (total - high.astype(F32)).astype(BF16)
    gathered = (dot(wbt_ref[...], high) + dot(wbt_ref[...], low)).astype(BF16)
    update = dot(gathered, wup_ref[...], TN)
    new = (emb_ref[...].astype(F32) + silu(update)).astype(BF16)
    new_ref[...] = new
    slope[...] = silu_slope(update)
    target = target_ref[...]
    shift = atom_dev.bit_length() - 1
    holder = lax.shift_right_logical(target, shift)
    line = lax.bitwise_and(holder, 1) * chips + lax.shift_right_logical(holder, 1)
    line = line * atom_dev + lax.bitwise_and(target, atom_dev - 1)
    parts[...] = dot(hot(line, parts.shape[0]), new).astype(BF16)
    pl.semaphore_wait(barrier, members - 1 + groups - 1)

    def pair_copy(k):
        c = chip_at(k)
        return send_to(
            some_rows(parts, theirs(c), atom_dev),
            some_rows(half, c, atom_dev),
            duo_send.at[0, k],
            duo_recv.at[0, k],
            graph=partner,
        )

    each(0, chips, lambda k: pair_copy(k).start())
    hot_of_ranks(wanted_ref, hots)

    def pair_sum(k):
        c = chip_at(k)
        pair_copy(k).wait_recv()
        return (
            some_rows(parts, mine(c), atom_dev)[...].astype(F32)
            + some_rows(half, c, atom_dev)[...].astype(F32)
        ).astype(BF16)

    def chip_copy(k):
        c = chip_at(k)
        return send_to(
            some_rows(pair, c, atom_dev), arrived.at[chip], far_send.at[0, k], far_recv.at[0, k], graph=2 * c + core
        )

    def pair_step(k):
        some_rows(pair, chip_at(k), atom_dev)[...] = pair_sum(k)
        chip_copy(k).start()

    each(1, chips, pair_step)
    arrived[chip] = pair_sum(0)
    each(1, chips, lambda k: chip_copy(k).wait_recv())

    asum = jnp.sum(arrived[...].astype(F32), axis=0).astype(BF16)
    pre = ATOM_SCALE * dot(asum, watom_ref[...])
    grad_pre = (gatom_ref[...].astype(F32) * silu_slope(pre)).astype(BF16)
    some_rows(grads, mine(chip), atom_dev)[...] = (
        ATOM_SCALE * dot(grad_pre, watom_ref[...], NT)
    ).astype(BF16)

    def grad_copy(k):
        rows = some_rows(grads, mine(chip), atom_dev)
        return send_to(rows, rows, far_send.at[1, k], far_recv.at[1, k], graph=2 * chip_at(k) + core)

    def grad_pass(k):
        rows = some_rows(grads, mine(chip_from(k)), atom_dev)
        return send_to(rows, rows, duo_send.at[1, k], duo_recv.at[1, k], graph=partner)

    def grad_forward(k):
        grad_copy(k).wait_recv()
        grad_pass(k).start()

    grad_pass(0).start()
    each(1, chips, lambda k: grad_copy(k).start())
    anew_ref[...] = (atom_ref[...].astype(F32) + silu(pre)).astype(BF16)
    wa[...] = (ATOM_SCALE * dot(asum, grad_pre, TN)).astype(BF16)
    each(1, chips, grad_forward)
    each(0, chips, lambda k: grad_pass(k).wait_recv())

    picked = dot(hot(line, grads.shape[0]), grads[...], TN)
    grad_new = gedge_ref[...].astype(F32) + picked
    gnew[...] = grad_new
    grad_update = (grad_new * slope[...]).astype(BF16)
    bil_wide = wbt_ref.shape[1]
    wb[:, bil_wide:] = dot(gathered, grad_update)
    gg = dot(wup_ref[...], grad_update, NT).astype(BF16)
    wb[:, :bil_wide] = dot(gg, high, NT) + dot(gg, low, NT)

    wa_rows = wa.shape[0] // members
    wb_rows = wb.shape[0] // 8
    wb_lanes = wb.shape[1] // NEAR
    wb_split = chips // NEAR

    def wb_tile(ref, c, base):
        return tile_of(ref, base * wb_split + lax.div(c, NEAR), wb_rows, lax.rem(c, NEAR), wb_lanes)

    def wa_duo():
        return send_to(
            some_rows(wa, other, wa.shape[0] // 2), wa_half, duo_send.at[2, 0], duo_recv.at[2, 0], graph=partner
        )

    def wb_duo():
        return send_to(
            some_rows(wb, other, wb.shape[0] // 2), wb_half, duo_send.at[2, 1], duo_recv.at[2, 1], graph=partner
        )

    def wa_far(k):
        c = chip_at(k)
        return send_to(
            some_rows(wa_pair, c, wa_rows), wa_in.at[chip], far_send.at[2, k], far_recv.at[2, k], graph=2 * c + core
        )

    def wb_far(k):
        c = chip_at(k)
        return send_to(
            wb_tile(wb_pair, c, 0), wb_in.at[chip], far_send.at[3, k], far_recv.at[3, k], graph=2 * c + core
        )

    def wa_group(k):
        peer = lax.rem(group + k, groups)
        return send_to(wa_dp.at[group], wa_dp.at[group], dp_send.at[0, k], dp_recv.at[0, k], dp=peer)

    def wb_group(k):
        peer = lax.rem(group + k, groups)
        return send_to(wb_dp.at[group], wb_dp.at[group], dp_send.at[1, k], dp_recv.at[1, k], dp=peer)

    def wa_back(k):
        rows = some_rows(wa_all, mine(chip), wa_rows)
        return send_to(rows, rows, far_send.at[4, k], far_recv.at[4, k], graph=2 * chip_at(k) + core)

    def wb_back(k):
        tile = wb_tile(wb_all, chip, core)
        return send_to(tile, tile, far_send.at[5, k], far_recv.at[5, k], graph=2 * chip_at(k) + core)

    def wa_pass(k):
        rows = some_rows(wa_all, mine(chip_from(k)), wa_rows)
        return send_to(rows, rows, duo_send.at[3, k], duo_recv.at[3, k], graph=partner)

    def wb_pass(k):
        tile = wb_tile(wb_all, chip_from(k), core)
        return send_to(tile, tile, duo_send.at[4, k], duo_recv.at[4, k], graph=partner)

    def sums_pair():
        wa_duo().wait_recv()
        wb_duo().wait_recv()
        wa_pair[...] = (
            some_rows(wa, core, wa.shape[0] // 2)[...].astype(F32) + wa_half[...].astype(F32)
        ).astype(BF16)
        wb_pair[...] = some_rows(wb, core, wb.shape[0] // 2)[...] + wb_half[...]

    def sums_far():
        def go(k):
            wa_far(k).start()
            wb_far(k).start()

        each(1, chips, go)
        wa_in[chip] = some_rows(wa_pair, chip, wa_rows)[...]
        wb_in[chip] = wb_tile(wb_pair, chip, 0)[...]

    def sums_group():
        def end(k):
            wa_far(k).wait_recv()
            wb_far(k).wait_recv()

        each(1, chips, end)
        wa_dp[group] = jnp.sum(wa_in[...].astype(F32), axis=0)
        wb_dp[group] = jnp.sum(wb_in[...], axis=0)

        def go(k):
            wa_group(k).start()
            wb_group(k).start()

        each(1, groups, go)

    def sums_back():
        def end(k):
            wa_group(k).wait_recv()
            wb_group(k).wait_recv()

        each(1, groups, end)
        some_rows(wa_all, mine(chip), wa_rows)[...] = (scale * jnp.sum(wa_dp[...], axis=0)).astype(BF16)
        wb_tile(wb_all, chip, core)[...] = scale * jnp.sum(wb_dp[...], axis=0)
        wa_pass(0).start()
        wb_pass(0).start()

        def go(k):
            wa_back(k).start()
            wb_back(k).start()

        each(1, chips, go)

    def sums_pass():
        def go(k):
            wa_back(k).wait_recv()
            wb_back(k).wait_recv()
            wa_pass(k).start()
            wb_pass(k).start()

        each(1, chips, go)

    wa_duo().start()
    wb_duo().start()

    block = math.gcd(slot_ref.shape[1], BLOCK)
    blocks = slot_ref.shape[1] // block
    far_shift = edges.bit_length() - 1 + NEAR.bit_length() - 1
    names[...] = jnp.zeros_like(names)
    acts = {1: sums_pair, 2: sums_far, 7: sums_group, 9: sums_back, 14: sums_pass}

    def triplets(i):
        for at, act in acts.items():
            pl.when(i == at * blocks // 16)(act)
        here = pl.ds(pl.multiple_of(i * block, block), block)
        at = i * block + lax.broadcasted_iota(jnp.int32, (1, block), 1)
        place = jnp.where(at < count_ref[0, 0], out_ref[:, here], -1)
        taken = dot(gg, hot(place, edges)).astype(BF16)
        backed = dot(wbil_ref[...], taken)
        basis = basis_ref[:, here].astype(F32)
        grad = basis[0:1, :] * backed[0:width]
        for b in range(1, basis.shape[0]):
            grad = grad + basis[b : b + 1, :] * backed[b * width : (b + 1) * width]
        source = lax.shift_right_logical(in_ref[:, here], far_shift)
        for k in range(far):
            spread[k * width : (k + 1) * width, :] = jnp.where(source == k, grad, 0.0).astype(BF16)
        names[...] += dot(spread[...], hot(slot_ref[:, here], names.shape[1]), NT)

    each(0, blocks, triplets)

    sent[...] = names[...].astype(BF16)

    def place(ref, index):
        return tile_of(ref, lax.div(index, NEAR), width, lax.rem(index, NEAR), CAP)

    def back_copy(k):
        peer = lax.rem(me + k, members)
        return send_to(
            place(sent, peer), some_lanes(back, me, CAP), far_send.at[6, k], far_recv.at[6, k], graph=peer
        )

    each(1, members, lambda k: back_copy(k).start())
    some_lanes(back, me, CAP)[...] = place(sent, me)[...]

    def sums_end(k):
        wa_pass(k).wait_recv()
        wb_pass(k).wait_recv()

    each(0, chips, sums_end)
    gat_ref[...] = wa_all[...].astype(F32)
    bil_ref[...] = wb_all[:, :bil_wide]
    up_ref[...] = wb_all[:, bil_wide:]
    each(1, members, lambda k: back_copy(k).wait_recv())
    grad = dot(back[...], hots[...])
    grad = (grad * silu_slope(proj_ref[...])).astype(BF16)

    wd[...] = dot(grad, emb_ref[...])

    def wd_tile(ref, index):
        return tile_of(ref, lax.div(index, NEAR), ref.shape[0] * NEAR // members, lax.rem(index, NEAR), LANES)

    def wd_far(k):
        peer = lax.rem(me + k, members)
        return send_to(wd_tile(wd, peer), wd_in.at[me], far_send.at[7, k], far_recv.at[7, k], graph=peer)

    def wd_group(k):
        peer = lax.rem(group + k, groups)
        return send_to(wd_dp.at[group], wd_dp.at[group], dp_send.at[2, k], dp_recv.at[2, k], dp=peer)

    def wd_back(k):
        tile = wd_tile(wd_all, me)
        return send_to(
            tile, tile, far_send.at[8, k], far_recv.at[8, k], graph=lax.rem(me + k, members)
        )

    each(1, members, lambda k: wd_far(k).start())
    wd_in[me] = wd_tile(wd, me)[...]
    gin_ref[...] = gnew[...] + dot(grad, wdt_ref[...], TN)
    each(1, members, lambda k: wd_far(k).wait_recv())
    wd_dp[group] = jnp.sum(wd_in[...], axis=0)
    each(1, groups, lambda k: wd_group(k).start())
    each(1, groups, lambda k: wd_group(k).wait_recv())
    wd_tile(wd_all, me)[...] = scale * jnp.sum(wd_dp[...], axis=0)
    each(1, members, lambda k: wd_back(k).start())

    def left(k):
        pair_copy(k).wait_send()
        grad_pass(k).wait_send()
        wa_pass(k).wait_send()
        wb_pass(k).wait_send()

    def left_far(k):
        chip_copy(k).wait_send()
        grad_copy(k).wait_send()
        wa_far(k).wait_send()
        wb_far(k).wait_send()
        wa_back(k).wait_send()
        wb_back(k).wait_send()

    def left_group(k):
        wa_group(k).wait_send()
        wb_group(k).wait_send()
        wd_group(k).wait_send()

    def left_all(k):
        back_copy(k).wait_send()
        wd_far(k).wait_send()

    each(0, chips, left)
    each(1, chips, left_far)
    each(1, groups, left_group)
    each(1, members, left_all)
    wa_duo().wait_send()
    wb_duo().wait_send()
    each(1, members, lambda k: wd_back(k).wait())
    down_ref[...] = wd_all[...]


def late(total, wbt, wup, emb, targets, watom, atom, gatom, gedge, slots, incoming, outgoing, count, basis, wbil, wanted, proj, wdt, members, groups, scale):
    edges, wide = emb.shape
    atom_dev = atom.shape[0]
    atoms = atom_dev * members
    width = wdt.shape[0]
    far = members // NEAR
    chips = members // 2
    block = math.gcd(slots.shape[1], BLOCK)
    all_wide = wbt.shape[1] + wide
    piece = (width // 8, all_wide // NEAR)
    wa_piece = (wide // members, wide)
    wd_piece = (width * NEAR // members, wide // NEAR)
    shape = jax.ShapeDtypeStruct
    return pl.pallas_call(
        functools.partial(late_kernel, members, groups, far, scale),
        out_shape=(
            shape((edges, wide), BF16),
            shape((atom_dev, wide), BF16),
            shape((edges, wide), F32),
            shape(wdt.shape, F32),
            shape(wbt.shape, F32),
            shape(wup.shape, F32),
            shape(watom.shape, F32),
        ),
        in_specs=[VMEM] * 12 + [pl.BlockSpec(memory_space=pltpu.SMEM)] + [VMEM] * 5,
        out_specs=(VMEM,) * 7,
        scratch_shapes=[
            pltpu.VMEM((atoms, wide), BF16),
            pltpu.VMEM((atoms // 2, wide), BF16),
            pltpu.VMEM((atoms // 2, wide), BF16),
            pltpu.VMEM((chips, atom_dev, wide), BF16),
            pltpu.VMEM((atoms, wide), BF16),
            pltpu.VMEM((edges, wide), F32),
            pltpu.VMEM((edges, wide), F32),
            pltpu.VMEM((wide, wide), BF16),
            pltpu.VMEM((wide // 2, wide), BF16),
            pltpu.VMEM((wide // 2, wide), BF16),
            pltpu.VMEM((chips, *wa_piece), BF16),
            pltpu.VMEM((groups, *wa_piece), F32),
            pltpu.VMEM((wide, wide), BF16),
            pltpu.VMEM((width, all_wide), F32),
            pltpu.VMEM((width // 2, all_wide), F32),
            pltpu.VMEM((width // 2, all_wide), F32),
            pltpu.VMEM((chips, *piece), F32),
            pltpu.VMEM((groups, *piece), F32),
            pltpu.VMEM((width, all_wide), F32),
            pltpu.VMEM((far * width, NEAR * CAP), F32),
            pltpu.VMEM((far * width, block), BF16),
            pltpu.VMEM((far * width, NEAR * CAP), BF16),
            pltpu.VMEM((width, members * CAP), BF16),
            pltpu.VMEM((members * CAP, edges), BF16),
            pltpu.VMEM((width, wide), F32),
            pltpu.VMEM((members, *wd_piece), F32),
            pltpu.VMEM((groups, *wd_piece), F32),
            pltpu.VMEM((width, wide), F32),
            pltpu.SemaphoreType.DMA((9, members)),
            pltpu.SemaphoreType.DMA((9, members)),
            pltpu.SemaphoreType.DMA((5, chips)),
            pltpu.SemaphoreType.DMA((5, chips)),
            pltpu.SemaphoreType.DMA((3, groups)),
            pltpu.SemaphoreType.DMA((3, groups)),
        ],
        compiler_params=params(collective_id=2, has_side_effects=True),
        name="late",
    )(total, wbt, wup, emb, targets, watom, atom, gatom, gedge, slots, incoming, outgoing, count, basis, wbil, wanted, proj, wdt)


def body(
    groups,
    members,
    edge_emb,
    atom_emb,
    edge_target,
    trip_in,
    trip_out,
    trip_count,
    trip_basis,
    grad_edge,
    grad_atom,
    w_down,
    w_bil,
    w_up,
    w_atom,
):
    emb = edge_emb[0]
    edges = emb.shape[0]
    wdt = w_down.T
    wbt = w_bil.T
    basis = trip_basis[0]
    wanted, slots, proj, table = early(trip_in, emb, wdt, members)
    total = forward(table, slots, trip_in, trip_out, trip_count, basis, edges)
    scale = 1.0 / math.sqrt(groups * members * edges)
    edge_new, atom_new, grad_in, down, bil, up, atom = late(
        total, wbt, w_up, emb, edge_target, w_atom, atom_emb[0], grad_atom[0], grad_edge[0],
        slots, trip_in, trip_out, trip_count, basis, w_bil, wanted, proj, wdt, members, groups, scale,
    )
    return (edge_new[None], atom_new[None], grad_in[None], down.T, bil.T, up, atom)


def solution(mesh):
    graph = P("dp", "graph")
    rows = P("dp", "graph", None)
    return jax.shard_map(
        functools.partial(body, mesh.shape["dp"], mesh.shape["graph"]),
        mesh=mesh,
        in_specs=(rows, rows, graph, graph, graph, graph, P("dp", None, "graph"), rows, rows)
        + (P(),) * 4,
        out_specs=(rows, rows, rows) + (P(),) * 4,
        check_vma=False,
    )
```

```python
import functools
import math

import jax
import jax.numpy as jnp
from jax import lax
from jax.experimental import pallas as pl
from jax.experimental.pallas import tpu as pltpu
from jax.sharding import PartitionSpec as P

MESH = pl.DeviceIdType.MESH
F32 = jnp.float32
BF16 = jnp.bfloat16
ATOM_SCALE = 0.25
CAP = 128
LANES = 128
NEAR_FORWARD = 2
NEAR_BACKWARD = 4
SPLIT = 4
BLOCK_NAMES = 2048
BLOCK_FORWARD = 2048
BLOCK_BACKWARD = 1024
ANY = pl.BlockSpec(memory_space=pl.ANY)
VMEM = pl.BlockSpec(memory_space=pltpu.VMEM)
NN = (((1,), (0,)), ((), ()))
NT = (((1,), (1,)), ((), ()))
TN = (((0,), (0,)), ((), ()))


def dot(a, b, dims=NN):
    return lax.dot_general(a, b, dims, preferred_element_type=F32)


def rows_of(shape):
    return lax.broadcasted_iota(jnp.int32, shape, 0)


def hot(index, size):
    return (rows_of((size, index.shape[1])) == index).astype(F32).astype(BF16)


def silu_slope(value):
    logistic = jax.nn.sigmoid(value)
    return logistic * (1.0 + value * (1.0 - logistic))


def silu(value):
    return value * jax.nn.sigmoid(value)


def params(**kw):
    return pltpu.CompilerParams(vmem_limit_bytes=60 * 1024 * 1024, **kw)


def send_to(src, dst, send, recv, **where):
    return pltpu.make_async_remote_copy(
        src_ref=src,
        dst_ref=dst,
        send_sem=send,
        recv_sem=recv,
        device_id=where,
        device_id_type=MESH,
    )


def drain(ref, sem):
    pltpu.make_async_copy(ref, ref, sem).wait()


def each(first, last, act, unroll=False):
    if unroll:
        for k in range(first, last):
            act(k)
        return

    def one(k, c):
        act(k)
        return c

    lax.fori_loop(first, last, one, 0)


def wrap(value, size):
    return jnp.where(value >= size, value - size, value)


def some_rows(ref, index, rows):
    return ref.at[pl.ds(pl.multiple_of(index * rows, rows), rows), :]


def some_lanes(ref, index, lanes):
    return ref.at[:, pl.ds(pl.multiple_of(index * lanes, lanes), lanes)]


def tile_of(ref, row, rows, lane, lanes):
    return ref.at[
        pl.ds(pl.multiple_of(row * rows, rows), rows),
        pl.ds(pl.multiple_of(lane * lanes, lanes), lanes),
    ]


def hot_of_ranks(rank_ref, hot_ref):
    members, per = rank_ref.shape[:2]
    place = lax.broadcasted_iota(jnp.int32, (CAP, LANES), 0).astype(F32)

    def one(d):
        ranks = rank_ref[d]
        at = pl.ds(pl.multiple_of(d * CAP, CAP), CAP)
        for q in range(per):
            hot_ref[at, q * LANES : (q + 1) * LANES] = (
                (place == ranks[q : q + 1, :]).astype(F32).astype(BF16)
            )

    each(0, members, one)


def block_kernel(members, groups, scale, names_of, *refs):
    r = dict(zip(names_of, refs))
    (in_ref, emb_ref, wdt_ref, wbt_ref, wup_ref, target_ref, atom_ref, gatom_ref, count_ref) = (
        r["incoming"], r["emb"], r["wdt"], r["wbt"], r["wup"], r["target"], r["atom"], r["gatom"], r["count"]
    )
    me = lax.axis_index("graph")
    group = lax.axis_index("dp")
    chips = members // 2
    chip = lax.div(me, 2)
    core = lax.rem(me, 2)
    other = 1 - core
    partner = 2 * chip + other
    all_send, all_recv, many_recv, dp_send, dp_recv, load = (
        r["all_send"], r["all_recv"], r["many_recv"], r["dp_send"], r["dp_recv"], r["load"]
    )

    def peer_at(k):
        return wrap(me + k, members)

    def chip_at(k):
        return wrap(chip + k, chips)

    def chip_from(k):
        return wrap(chip + chips - k, chips)

    def group_at(k):
        return wrap(group + k, groups)

    def mine(c):
        return core * chips + c

    loads = [
        pltpu.make_async_copy(r[name + "_hbm"], r[name], load.at[i])
        for i, name in enumerate(("outgoing", "basis", "watom", "gedge"))
    ]
    for one in loads:
        one.start()
    barrier = pltpu.get_barrier_semaphore()
    each(
        1,
        members,
        lambda k: pl.semaphore_signal(
            barrier, inc=1, device_id={"graph": peer_at(k)}, device_id_type=MESH
        ),
        True,
    )
    each(
        1,
        groups,
        lambda k: pl.semaphore_signal(
            barrier, inc=1, device_id={"dp": group_at(k)}, device_id_type=MESH
        ),
        True,
    )

    table, found, rank_buf, wanted, hots, chosen, name, features = (
        r["table"], r["found"], r["rank_buf"], r["wanted"], r["hots"], r["chosen"], r["name"], r["features"]
    )
    highs = table.shape[0]
    per = highs // members
    width = wdt_ref.shape[0]
    edges, wide = emb_ref.shape
    slots = in_ref.shape[1]
    nblock = math.gcd(slots, BLOCK_NAMES)

    def window(i, block):
        return pl.ds(pl.multiple_of(i * block, block), block)

    def parts_of(i):
        index = in_ref[:, window(i, nblock)]
        return lax.shift_right_logical(index, 7), lax.bitwise_and(index, LANES - 1)

    found[...] = jnp.zeros_like(found)

    def find(i):
        high, low = parts_of(i)
        found[...] += dot(hot(high, highs), hot(low, LANES), NT)

    each(0, slots // nblock, find)
    there = jnp.where(found[...] > 0.0, 1.0, 0.0)
    there16 = there.astype(BF16)
    row = lax.broadcasted_iota(jnp.int32, (LANES, LANES), 0)
    col = lax.broadcasted_iota(jnp.int32, (LANES, LANES), 1)
    upper = (row <= col).astype(F32).astype(BF16)
    hrow = lax.broadcasted_iota(jnp.int32, (highs, highs), 0)
    hcol = lax.broadcasted_iota(jnp.int32, (highs, highs), 1)
    before = ((hcol < hrow) & (lax.div(hcol, per) == lax.div(hrow, per))).astype(F32).astype(BF16)
    ahead = dot(before, there16).astype(BF16)
    ones = jnp.ones((LANES, LANES), BF16)
    rank = dot(there16, upper) + dot(ahead, ones) - 1.0
    rank = jnp.where(there > 0.0, rank, -1.0)
    table[...] = rank.astype(BF16)
    for s in range(members):
        rank_buf[s] = rank[s * per : (s + 1) * per, :]
    proj = dot(wdt_ref[...], emb_ref[...], NT)
    feat = silu(proj).astype(BF16)
    r["down_slope"][...] = silu_slope(proj)
    pl.semaphore_wait(barrier, members - 1 + groups - 1)

    def rank_copy(k):
        peer = peer_at(k)
        return send_to(rank_buf.at[peer], wanted.at[me], all_send.at[0], all_recv.at[0], graph=peer)

    each(1, members, lambda k: rank_copy(k).start(), True)
    wanted[me] = rank_buf[me]

    def look(i):
        high, low = parts_of(i)
        ranks = dot(table[...], hot(high, highs), TN)
        picked = jnp.where(rows_of(ranks.shape) == low, ranks, 0.0)
        rank = jnp.sum(picked, axis=0, keepdims=True).astype(jnp.int32)
        name[:, window(i, nblock)] = lax.div(high, per) * CAP + rank

    looks = slots // nblock
    each(0, looks // 2, look)
    drain(wanted.at[0 : members - 1], all_recv.at[0])
    hot_of_ranks(wanted, hots)
    chosen[...] = dot(feat, hots[...], NT).astype(BF16)

    def feature_tile(index):
        return tile_of(
            features, lax.div(index, NEAR_FORWARD), width, lax.rem(index, NEAR_FORWARD), CAP
        )

    def feature_copy(k):
        peer = peer_at(k)
        return send_to(
            some_lanes(chosen, peer, CAP), feature_tile(me), all_send.at[1], all_recv.at[1], graph=peer
        )

    each(1, members, lambda k: feature_copy(k).start(), True)
    feature_tile(me)[...] = some_lanes(chosen, me, CAP)[...]
    each(looks // 2, looks, look)
    r["wbil"][...] = wbt_ref[...].astype(F32).T.astype(BF16)
    drain(chosen.at[:, 0 : (members - 1) * CAP], all_recv.at[1])
    loads[0].wait()
    loads[1].wait()

    outgoing, basis_ref, spread, total_ref = r["outgoing"], r["basis"], r["spread"], r["total"]
    fblock = math.gcd(slots, BLOCK_FORWARD)
    far_shift = (NEAR_FORWARD * CAP).bit_length() - 1
    far = members // NEAR_FORWARD
    total_ref[...] = jnp.zeros_like(total_ref)

    def place_of(i, block):
        at = i * block + lax.broadcasted_iota(jnp.int32, (1, block), 1)
        return jnp.where(at < count_ref[0, 0], outgoing[:, window(i, block)], -1)

    def forward(i):
        here = window(i, fblock)
        index = name[:, here]
        group_of = lax.shift_right_logical(index, far_shift)
        all_wide = dot(features[...], hot(lax.bitwise_and(index, NEAR_FORWARD * CAP - 1), NEAR_FORWARD * CAP))
        feat = all_wide[0:width]
        for k in range(1, far):
            feat = jnp.where(group_of == k, all_wide[k * width : (k + 1) * width], feat)
        basis = basis_ref[:, here].astype(F32)
        for b in range(basis.shape[0]):
            spread[b * width : (b + 1) * width, :] = (basis[b : b + 1, :] * feat).astype(BF16)
        total_ref[...] += dot(spread[...], hot(place_of(i, fblock), edges), NT)

    each(0, slots // fblock, forward)

    parts, half, pair, arrived, grads, slope, gnew = (
        r["parts"], r["half"], r["pair"], r["arrived"], r["grads"], r["slope"], r["gnew"]
    )
    new_ref, anew_ref = r["new_out"], r["anew_out"]
    atom_dev = atom_ref.shape[0]
    total = total_ref[...]
    high = total.astype(BF16)
    low = (total - high.astype(F32)).astype(BF16)
    gathered = (dot(wbt_ref[...], high) + dot(wbt_ref[...], low)).astype(BF16)
    target = target_ref[...]
    holder = lax.shift_right_logical(target, atom_dev.bit_length() - 1)
    line = lax.bitwise_and(holder, 1) * chips + lax.shift_right_logical(holder, 1)
    line = line * atom_dev + lax.bitwise_and(target, atom_dev - 1)
    line_hot = hot(line, parts.shape[0])
    part = wide // SPLIT

    def pair_copy(q):
        rows = parts.shape[0] // 2
        lanes = slice(q * part, (q + 1) * part)
        return send_to(
            parts.at[pl.ds(pl.multiple_of(other * rows, rows), rows), lanes],
            half.at[:, lanes],
            all_send.at[2],
            many_recv.at[0, q],
            graph=partner,
        )

    for q in range(SPLIT):
        lanes = slice(q * part, (q + 1) * part)
        update = dot(gathered, wup_ref[:, lanes], TN)
        new = (emb_ref[:, lanes].astype(F32) + silu(update)).astype(BF16)
        new_ref[:, lanes] = new
        slope[:, lanes] = silu_slope(update)
        parts[:, lanes] = dot(line_hot, new).astype(BF16)
        pair_copy(q).start()

    def chip_copy(k):
        c = chip_at(k)
        return send_to(
            some_rows(pair, c, atom_dev), arrived.at[chip], all_send.at[3], all_recv.at[3], graph=2 * c + core
        )

    for q in range(SPLIT):
        lanes = slice(q * part, (q + 1) * part)
        rows = parts.shape[0] // 2
        own = parts[pl.ds(pl.multiple_of(core * rows, rows), rows), lanes].astype(F32)
        pair_copy(q).wait_recv()
        pair[:, lanes] = (own + half[:, lanes].astype(F32)).astype(BF16)
    each(1, chips, lambda k: chip_copy(k).start(), True)
    arrived[chip] = some_rows(pair, chip, atom_dev)[...]
    loads[2].wait()
    loads[3].wait()
    watom_ref, gedge_ref = r["watom"], r["gedge"]
    drain(arrived.at[0 : chips - 1], all_recv.at[3])

    asum = jnp.sum(arrived[...].astype(F32), axis=0).astype(BF16)
    pre = ATOM_SCALE * dot(asum, watom_ref[...])
    grad_pre = (gatom_ref[...].astype(F32) * silu_slope(pre)).astype(BF16)
    some_rows(grads, mine(chip), atom_dev)[...] = (
        ATOM_SCALE * dot(grad_pre, watom_ref[...], NT)
    ).astype(BF16)

    def grad_copy(k):
        rows = some_rows(grads, mine(chip), atom_dev)
        return send_to(rows, rows, all_send.at[4], many_recv.at[1, k], graph=2 * chip_at(k) + core)

    def grad_pass(k):
        rows = some_rows(grads, mine(chip_from(k)), atom_dev)
        return send_to(rows, rows, all_send.at[5], all_recv.at[5], graph=partner)

    def grad_forward(k):
        grad_copy(k).wait_recv()
        grad_pass(k).start()

    each(1, chips, lambda k: grad_copy(k).start(), True)
    grad_pass(0).start()
    wa, wb = r["wa"], r["wb"]
    anew_ref[...] = (atom_ref[...].astype(F32) + silu(pre)).astype(BF16)
    wa[...] = (ATOM_SCALE * dot(asum, grad_pre, TN)).astype(BF16)
    each(1, chips, grad_forward, True)
    drain(half, all_recv.at[5])

    picked = dot(hot(line, grads.shape[0]), grads[...], TN)
    grad_new = gedge_ref[...].astype(F32) + picked
    gnew[...] = grad_new
    grad_update = (grad_new * slope[...]).astype(BF16)
    bil_wide = wbt_ref.shape[1]
    wb[:, bil_wide:] = dot(gathered, grad_update)
    gg = dot(wup_ref[...], grad_update, NT).astype(BF16)
    wb[:, :bil_wide] = dot(gg, high, NT) + dot(gg, low, NT)

    wa_half, wa_pair, wa_in, wa_dp, wa_all = r["wa_half"], r["wa_pair"], r["wa_in"], r["wa_dp"], r["wa_out"]
    wb_half, wb_pair, wb_in, wb_dp, wb_all = r["wb_half"], r["wb_pair"], r["wb_in"], r["wb_dp"], r["wb_out"]
    wa_rows = wa.shape[0] // members
    wb_rows = wb.shape[0] // 8
    wb_lanes = wb.shape[1] // SPLIT
    wb_split = chips // SPLIT

    def wb_tile(ref, c, base):
        return tile_of(ref, base * wb_split + lax.div(c, SPLIT), wb_rows, lax.rem(c, SPLIT), wb_lanes)

    def wa_duo():
        return send_to(
            some_rows(wa, other, wa.shape[0] // 2), wa_half, all_send.at[6], all_recv.at[6], graph=partner
        )

    def wb_duo():
        return send_to(
            some_rows(wb, other, wb.shape[0] // 2), wb_half, all_send.at[7], all_recv.at[7], graph=partner
        )

    def wa_far(k):
        c = chip_at(k)
        return send_to(
            some_rows(wa_pair, c, wa_rows), wa_in.at[chip], all_send.at[8], all_recv.at[8], graph=2 * c + core
        )

    def wb_far(k):
        c = chip_at(k)
        return send_to(
            wb_tile(wb_pair, c, 0), wb_in.at[chip], all_send.at[9], all_recv.at[9], graph=2 * c + core
        )

    def wa_group(k):
        return send_to(wa_dp.at[group], wa_dp.at[group], dp_send.at[0], dp_recv.at[0], dp=group_at(k))

    def wb_group(k):
        return send_to(wb_dp.at[group], wb_dp.at[group], dp_send.at[1], dp_recv.at[1], dp=group_at(k))

    def wa_back(k):
        rows = some_rows(wa_all, mine(chip), wa_rows)
        return send_to(rows, rows, all_send.at[10], all_recv.at[10], graph=2 * chip_at(k) + core)

    def wb_back(k):
        tile = wb_tile(wb_all, chip, core)
        return send_to(tile, tile, all_send.at[11], all_recv.at[11], graph=2 * chip_at(k) + core)

    def wa_pass():
        rows = some_rows(wa_all, core, wa.shape[0] // 2)
        return send_to(rows, rows, all_send.at[12], all_recv.at[12], graph=partner)

    def wb_pass():
        rows = some_rows(wb_all, core, wb.shape[0] // 2)
        return send_to(rows, rows, all_send.at[13], all_recv.at[13], graph=partner)

    def sums_pair():
        wa_duo().wait_recv()
        wb_duo().wait_recv()
        wa_pair[...] = (
            some_rows(wa, core, wa.shape[0] // 2)[...].astype(F32) + wa_half[...].astype(F32)
        ).astype(BF16)
        wb_pair[...] = some_rows(wb, core, wb.shape[0] // 2)[...] + wb_half[...]

    def sums_far():
        def go(k):
            wa_far(k).start()
            wb_far(k).start()

        each(1, chips, go, True)
        wa_in[chip] = some_rows(wa_pair, chip, wa_rows)[...]
        wb_in[chip] = wb_tile(wb_pair, chip, 0)[...]

    def sums_group():
        drain(wa_in.at[0 : chips - 1], all_recv.at[8])
        drain(wb_in.at[0 : chips - 1], all_recv.at[9])
        wa_dp[group] = jnp.sum(wa_in[...].astype(F32), axis=0)
        wb_dp[group] = jnp.sum(wb_in[...], axis=0)

        def go(k):
            wa_group(k).start()
            wb_group(k).start()

        each(1, groups, go, True)

    def sums_back():
        drain(wa_dp.at[0 : groups - 1], dp_recv.at[0])
        drain(wb_dp.at[0 : groups - 1], dp_recv.at[1])
        some_rows(wa_all, mine(chip), wa_rows)[...] = (scale * jnp.sum(wa_dp[...], axis=0)).astype(BF16)
        wb_tile(wb_all, chip, core)[...] = scale * jnp.sum(wb_dp[...], axis=0)

        def go(k):
            wa_back(k).start()
            wb_back(k).start()

        each(1, chips, go, True)

    def sums_pass():
        drain(wa_in.at[0 : chips - 1], all_recv.at[10])
        drain(wb_in.at[0 : chips - 1], all_recv.at[11])
        wa_pass().start()
        wb_pass().start()

    wa_duo().start()
    wb_duo().start()

    sent, back = r["sent"], r["back"]
    named, masked, wbil = r["named"], r["masked"], r["wbil"]
    block = math.gcd(slots, BLOCK_BACKWARD)
    blocks = slots // block
    back_far = members // NEAR_BACKWARD
    back_shift = (NEAR_BACKWARD * CAP).bit_length() - 1
    named[...] = jnp.zeros_like(named)
    acts = {1: sums_pair, 2: sums_far, 7: sums_group, 9: sums_back, 14: sums_pass}

    def backward(i):
        for at, act in acts.items():
            pl.when(i == at * blocks // 16)(act)
        here = window(i, block)
        taken = dot(gg, hot(place_of(i, block), edges)).astype(BF16)
        backed = dot(wbil[...], taken)
        basis = basis_ref[:, here].astype(F32)
        grad = basis[0:1, :] * backed[0:width]
        for b in range(1, basis.shape[0]):
            grad = grad + basis[b : b + 1, :] * backed[b * width : (b + 1) * width]
        index = name[:, here]
        source = lax.shift_right_logical(index, back_shift)
        for k in range(back_far):
            masked[k * width : (k + 1) * width, :] = jnp.where(source == k, grad, 0.0).astype(BF16)
        near = lax.bitwise_and(index, NEAR_BACKWARD * CAP - 1)
        named[...] += dot(masked[...], hot(near, NEAR_BACKWARD * CAP), NT)

    each(0, blocks, backward)

    sent[...] = named[...].astype(BF16)

    def sent_tile(index):
        return tile_of(sent, lax.div(index, NEAR_BACKWARD), width, lax.rem(index, NEAR_BACKWARD), CAP)

    def back_copy(k):
        peer = peer_at(k)
        return send_to(
            sent_tile(peer), some_lanes(back, me, CAP), all_send.at[14], all_recv.at[14], graph=peer
        )

    each(1, members, lambda k: back_copy(k).start(), True)
    some_lanes(back, me, CAP)[...] = sent_tile(me)[...]
    wa_pass().wait_recv()
    wb_pass().wait_recv()
    drain(back.at[:, 0 : (members - 1) * CAP], all_recv.at[14])
    grad = dot(back[...], hots[...])
    grad = (grad * r["down_slope"][...]).astype(BF16)

    wd, wd_in, wd_dp, wd_all = r["wd"], r["wd_in"], r["wd_dp"], r["wd_out"]
    wd[...] = dot(grad, emb_ref[...])

    def wd_tile(ref, index):
        return tile_of(ref, lax.div(index, SPLIT), ref.shape[0] * SPLIT // members, lax.rem(index, SPLIT), LANES)

    def wd_far(k):
        peer = peer_at(k)
        return send_to(wd_tile(wd, peer), wd_in.at[me], all_send.at[15], all_recv.at[15], graph=peer)

    def wd_group(k):
        return send_to(wd_dp.at[group], wd_dp.at[group], dp_send.at[2], dp_recv.at[2], dp=group_at(k))

    def wd_back(k):
        tile = wd_tile(wd_all, me)
        return send_to(tile, tile, all_send.at[16], all_recv.at[16], graph=peer_at(k))

    each(1, members, lambda k: wd_far(k).start(), True)
    wd_in[me] = wd_tile(wd, me)[...]
    r["gin_out"][...] = gnew[...] + dot(grad, wdt_ref[...], TN)
    drain(wd_in.at[0 : members - 1], all_recv.at[15])
    wd_dp[group] = jnp.sum(wd_in[...], axis=0)
    each(1, groups, lambda k: wd_group(k).start(), True)
    drain(wd_dp.at[0 : groups - 1], dp_recv.at[2])
    wd_tile(wd_all, me)[...] = scale * jnp.sum(wd_dp[...], axis=0)
    each(1, members, lambda k: wd_back(k).start(), True)

    drain(wanted.at[0 : members - 1], all_send.at[0])
    drain(chosen.at[:, 0 : (members - 1) * CAP], all_send.at[1])
    drain(half, all_send.at[2])
    drain(arrived.at[0 : chips - 1], all_send.at[3])
    drain(arrived.at[0 : chips - 1], all_send.at[4])
    drain(half, all_send.at[5])
    wa_duo().wait_send()
    wb_duo().wait_send()
    drain(wa_in.at[0 : chips - 1], all_send.at[8])
    drain(wb_in.at[0 : chips - 1], all_send.at[9])
    drain(wa_in.at[0 : chips - 1], all_send.at[10])
    drain(wb_in.at[0 : chips - 1], all_send.at[11])
    wa_pass().wait_send()
    wb_pass().wait_send()
    drain(wa_dp.at[0 : groups - 1], dp_send.at[0])
    drain(wb_dp.at[0 : groups - 1], dp_send.at[1])
    drain(wd_dp.at[0 : groups - 1], dp_send.at[2])
    drain(back.at[:, 0 : (members - 1) * CAP], all_send.at[14])
    drain(wd_in.at[0 : members - 1], all_send.at[15])
    drain(wd_in.at[0 : members - 1], all_send.at[16])
    drain(wd_in.at[0 : members - 1], all_recv.at[16])


def block_of(values, members, groups, scale):
    shape = jax.ShapeDtypeStruct
    edges, wide = values["emb"].shape
    atom_dev = values["atom"].shape[0]
    atoms = atom_dev * members
    width = values["wdt"].shape[0]
    slots = values["incoming"].shape[1]
    rows = values["wbt"].shape[1]
    chips = members // 2
    highs = members * edges // LANES
    per = highs // members
    all_wide = rows + wide
    piece = (width // 8, all_wide // SPLIT)
    wa_piece = (wide // members, wide)
    wd_piece = (width * SPLIT // members, wide // SPLIT)
    far = members // NEAR_FORWARD
    back_far = members // NEAR_BACKWARD
    late = ("outgoing", "basis", "watom", "gedge")
    ins, specs, args = [], [], []
    for key, value in values.items():
        if key in late:
            ins.append(key + "_hbm")
            specs.append(ANY)
        else:
            ins.append(key)
            specs.append(pl.BlockSpec(memory_space=pltpu.SMEM) if key == "count" else VMEM)
        args.append(value)
    outs = {
        "new_out": shape((edges, wide), BF16),
        "anew_out": shape((atom_dev, wide), BF16),
        "gin_out": shape((edges, wide), F32),
        "wa_out": shape((wide, wide), BF16),
        "wb_out": shape((width, all_wide), F32),
        "wd_out": shape((width, wide), F32),
    }
    scratch = {key: pltpu.VMEM(values[key].shape, values[key].dtype) for key in late}
    scratch |= {
        "table": pltpu.VMEM((highs, LANES), BF16),
        "found": pltpu.VMEM((highs, LANES), F32),
        "rank_buf": pltpu.VMEM((members, per, LANES), F32),
        "wanted": pltpu.VMEM((members, per, LANES), F32),
        "hots": pltpu.VMEM((members * CAP, edges), BF16),
        "chosen": pltpu.VMEM((width, members * CAP), BF16),
        "name": pltpu.VMEM((1, slots), jnp.int32),
        "features": pltpu.VMEM((far * width, NEAR_FORWARD * CAP), BF16),
        "down_slope": pltpu.VMEM((width, edges), F32),
        "wbil": pltpu.VMEM((rows, width), BF16),
        "spread": pltpu.VMEM((rows, math.gcd(slots, BLOCK_FORWARD)), BF16),
        "total": pltpu.VMEM((rows, edges), F32),
        "parts": pltpu.VMEM((atoms, wide), BF16),
        "half": pltpu.VMEM((atoms // 2, wide), BF16),
        "pair": pltpu.VMEM((atoms // 2, wide), BF16),
        "arrived": pltpu.VMEM((chips, atom_dev, wide), BF16),
        "grads": pltpu.VMEM((atoms, wide), BF16),
        "slope": pltpu.VMEM((edges, wide), F32),
        "gnew": pltpu.VMEM((edges, wide), F32),
        "wa": pltpu.VMEM((wide, wide), BF16),
        "wa_half": pltpu.VMEM((wide // 2, wide), BF16),
        "wa_pair": pltpu.VMEM((wide // 2, wide), BF16),
        "wa_in": pltpu.VMEM((chips, *wa_piece), BF16),
        "wa_dp": pltpu.VMEM((groups, *wa_piece), F32),
        "wb": pltpu.VMEM((width, all_wide), F32),
        "wb_half": pltpu.VMEM((width // 2, all_wide), F32),
        "wb_pair": pltpu.VMEM((width // 2, all_wide), F32),
        "wb_in": pltpu.VMEM((chips, *piece), F32),
        "wb_dp": pltpu.VMEM((groups, *piece), F32),
        "named": pltpu.VMEM((back_far * width, NEAR_BACKWARD * CAP), F32),
        "masked": pltpu.VMEM((back_far * width, math.gcd(slots, BLOCK_BACKWARD)), BF16),
        "sent": pltpu.VMEM((back_far * width, NEAR_BACKWARD * CAP), BF16),
        "back": pltpu.VMEM((width, members * CAP), BF16),
        "wd": pltpu.VMEM((width, wide), F32),
        "wd_in": pltpu.VMEM((members, *wd_piece), F32),
        "wd_dp": pltpu.VMEM((groups, *wd_piece), F32),
        "all_send": pltpu.SemaphoreType.DMA((17,)),
        "all_recv": pltpu.SemaphoreType.DMA((17,)),
        "many_recv": pltpu.SemaphoreType.DMA((2, chips)),
        "dp_send": pltpu.SemaphoreType.DMA((3,)),
        "dp_recv": pltpu.SemaphoreType.DMA((3,)),
        "load": pltpu.SemaphoreType.DMA((4,)),
    }
    return pl.pallas_call(
        functools.partial(block_kernel, members, groups, scale, (*ins, *outs, *scratch)),
        out_shape=tuple(outs.values()),
        in_specs=specs,
        out_specs=(VMEM,) * len(outs),
        scratch_shapes=list(scratch.values()),
        compiler_params=params(collective_id=1, has_side_effects=True),
        name="block",
    )(*args)


def finish_kernel(*refs):
    new, anew, gin, wa, wb, wd, new_o, anew_o, gin_o, down_o, bil_o, up_o, gat_o = refs
    new_o[...] = new[...]
    anew_o[...] = anew[...]
    gin_o[...] = gin[...]
    down_o[...] = wd[...]
    bil_o[...] = wb[:, : bil_o.shape[1]]
    up_o[...] = wb[:, bil_o.shape[1] :]
    gat_o[...] = wa[...].astype(F32)


def finish(new, anew, gin, wa, wb, wd):
    shape = jax.ShapeDtypeStruct
    wide = wa.shape[1]
    width = wb.shape[0]
    return pl.pallas_call(
        finish_kernel,
        out_shape=(
            shape(new.shape, BF16),
            shape(anew.shape, BF16),
            shape(gin.shape, F32),
            shape(wd.shape, F32),
            shape((width, wb.shape[1] - wide), F32),
            shape((width, wide), F32),
            shape(wa.shape, F32),
        ),
        in_specs=[VMEM] * 6,
        out_specs=(VMEM,) * 7,
        compiler_params=params(),
        name="finish",
    )(new, anew, gin, wa, wb, wd)


def body(
    groups,
    members,
    edge_emb,
    atom_emb,
    edge_target,
    trip_in,
    trip_out,
    trip_count,
    trip_basis,
    grad_edge,
    grad_atom,
    w_down,
    w_bil,
    w_up,
    w_atom,
):
    scale = 1.0 / math.sqrt(groups * members * edge_emb.shape[1])
    values = dict(
        incoming=trip_in,
        emb=edge_emb[0],
        wdt=w_down.T,
        wbt=w_bil.T,
        wup=w_up,
        target=edge_target,
        atom=atom_emb[0],
        gatom=grad_atom[0],
        count=trip_count,
        outgoing=trip_out,
        basis=trip_basis[0],
        watom=w_atom,
        gedge=grad_edge[0],
    )
    edge_new, atom_new, grad_in, down, bil, up, atom = finish(*block_of(values, members, groups, scale))
    return (edge_new[None], atom_new[None], grad_in[None], down.T, bil.T, up, atom)


def solution(mesh):
    graph = P("dp", "graph")
    rows = P("dp", "graph", None)
    return jax.shard_map(
        functools.partial(body, mesh.shape["dp"], mesh.shape["graph"]),
        mesh=mesh,
        in_specs=(rows, rows, graph, graph, graph, graph, P("dp", None, "graph"), rows, rows)
        + (P(),) * 4,
        out_specs=(rows, rows, rows) + (P(),) * 4,
        check_vma=False,
    )
```

```python
import functools
import math

import jax
import jax.numpy as jnp
from jax import lax
from jax.experimental import pallas as pl
from jax.experimental.pallas import tpu as pltpu
from jax.sharding import PartitionSpec as P

MESH = pl.DeviceIdType.MESH
F32 = jnp.float32
HALVES = 2
TURNS = 4
BF16 = jnp.bfloat16
ATOM_SCALE = 0.25
CAP = 128
LANES = 128
NEAR_FORWARD = 2
NEAR_BACKWARD = 4
SPLIT = 4
BLOCK_NAMES = 4096
BLOCK_FORWARD = 2048
BLOCK_BACKWARD = 1024
ANY = pl.BlockSpec(memory_space=pl.ANY)
VMEM = pl.BlockSpec(memory_space=pltpu.VMEM)
NN = (((1,), (0,)), ((), ()))
NT = (((1,), (1,)), ((), ()))
TN = (((0,), (0,)), ((), ()))


def dot(a, b, dims=NN):
    return lax.dot_general(a, b, dims, preferred_element_type=F32)


def rows_of(shape):
    return lax.broadcasted_iota(jnp.int32, shape, 0)


def hot(index, size):
    return (rows_of((size, index.shape[1])) == index).astype(F32).astype(BF16)


def silu_slope(value):
    logistic = jax.nn.sigmoid(value)
    return logistic * (1.0 + value * (1.0 - logistic))


def silu(value):
    return value * jax.nn.sigmoid(value)


def params(**kw):
    return pltpu.CompilerParams(vmem_limit_bytes=60 * 1024 * 1024, **kw)


def send_to(src, dst, send, recv, **where):
    return pltpu.make_async_remote_copy(
        src_ref=src,
        dst_ref=dst,
        send_sem=send,
        recv_sem=recv,
        device_id=where,
        device_id_type=MESH,
    )


def drain(ref, sem):
    pltpu.make_async_copy(ref, ref, sem).wait()


def each(first, last, act, unroll=False):
    if unroll:
        for k in range(first, last):
            act(k)
        return

    def one(k, c):
        act(k)
        return c

    lax.fori_loop(first, last, one, 0)


def wrap(value, size):
    return jnp.where(value >= size, value - size, value)


def some_rows(ref, index, rows):
    return ref.at[pl.ds(pl.multiple_of(index * rows, rows), rows), :]


def tile_of(ref, row, rows, lane, lanes):
    return ref.at[
        pl.ds(pl.multiple_of(row * rows, rows), rows),
        pl.ds(pl.multiple_of(lane * lanes, lanes), lanes),
    ]


def hot_of_ranks(rank_ref, hot_ref, first, last):
    per = rank_ref.shape[1]
    place = lax.broadcasted_iota(jnp.int32, (CAP, LANES), 0).astype(F32)

    def one(d):
        ranks = rank_ref[d]
        at = pl.ds(pl.multiple_of(d * CAP, CAP), CAP)
        for q in range(per):
            hot_ref[at, q * LANES : (q + 1) * LANES] = (
                (place == ranks[q : q + 1, :]).astype(F32).astype(BF16)
            )

    each(first, last, one)


def block_kernel(members, groups, scale, names_of, *refs):
    r = dict(zip(names_of, refs))
    (in_ref, emb_ref, wdt_ref, wbt_ref, wup_ref, target_ref, atom_ref, gatom_ref, count_ref) = (
        r["incoming"], r["emb"], r["wdt"], r["wbt"], r["wup"], r["target"], r["atom"], r["gatom"], r["count"]
    )
    me = lax.axis_index("graph")
    group = lax.axis_index("dp")
    chips = members // 2
    chip = lax.div(me, 2)
    core = lax.rem(me, 2)
    other = 1 - core
    partner = 2 * chip + other
    all_send, all_recv, many_recv, dp_send, dp_recv, load = (
        r["all_send"], r["all_recv"], r["many_recv"], r["dp_send"], r["dp_recv"], r["load"]
    )

    def peer_at(k):
        return wrap(me + k, members)

    def chip_at(k):
        return wrap(chip + k, chips)

    def chip_from(k):
        return wrap(chip + chips - k, chips)

    def group_at(k):
        return wrap(group + k, groups)

    def mine(c):
        return core * chips + c

    loads = [
        pltpu.make_async_copy(r[name + "_hbm"], r[name], load.at[i])
        for i, name in enumerate(("outgoing", "basis", "watom", "gedge"))
    ]
    for one in loads:
        one.start()
    barrier = pltpu.get_barrier_semaphore()
    each(
        1,
        members,
        lambda k: pl.semaphore_signal(
            barrier, inc=1, device_id={"graph": peer_at(k)}, device_id_type=MESH
        ),
        True,
    )
    each(
        1,
        groups,
        lambda k: pl.semaphore_signal(
            barrier, inc=1, device_id={"dp": group_at(k)}, device_id_type=MESH
        ),
        True,
    )

    table, found, rank_buf, wanted, hots, chosen, name, features = (
        r["table"], r["found"], r["rank_buf"], r["wanted"], r["hots"], r["chosen"], r["name"], r["features"]
    )
    highs = table.shape[0]
    per = highs // members
    width = wdt_ref.shape[0]
    edges, wide = emb_ref.shape
    slots = in_ref.shape[1]
    nblock = math.gcd(slots, BLOCK_NAMES)

    def window(i, block):
        return pl.ds(pl.multiple_of(i * block, block), block)

    def parts_of(i):
        index = in_ref[:, window(i, nblock)]
        return lax.shift_right_logical(index, 7), lax.bitwise_and(index, LANES - 1)

    found[...] = jnp.zeros_like(found)

    def find(i):
        high, low = parts_of(i)
        found[...] += dot(hot(high, highs), hot(low, LANES), NT)

    each(0, slots // nblock, find)
    there = jnp.where(found[...] > 0.0, 1.0, 0.0)
    there16 = there.astype(BF16)
    row = lax.broadcasted_iota(jnp.int32, (LANES, LANES), 0)
    col = lax.broadcasted_iota(jnp.int32, (LANES, LANES), 1)
    upper = (row <= col).astype(F32).astype(BF16)
    hrow = lax.broadcasted_iota(jnp.int32, (highs, highs), 0)
    hcol = lax.broadcasted_iota(jnp.int32, (highs, highs), 1)
    before = ((hcol < hrow) & (lax.div(hcol, per) == lax.div(hrow, per))).astype(F32).astype(BF16)
    ahead = dot(before, there16).astype(BF16)
    ones = jnp.ones((LANES, LANES), BF16)
    rank = dot(there16, upper) + dot(ahead, ones) - 1.0
    rank = jnp.where(there > 0.0, rank, -1.0)
    table[...] = rank.astype(BF16)
    for s in range(members):
        rank_buf[s] = rank[s * per : (s + 1) * per, :]
    proj = dot(wdt_ref[...], emb_ref[...], NT)
    feat = silu(proj).astype(BF16)
    r["down_slope"][...] = silu_slope(proj)
    pl.semaphore_wait(barrier, members - 1 + groups - 1)

    def rank_copy(k):
        peer = peer_at(k)
        return send_to(
            rank_buf.at[peer], wanted.at[members - k], all_send.at[0], all_recv.at[0], graph=peer
        )

    each(1, members, lambda k: rank_copy(k).start(), True)
    wanted[0] = rank_buf[me]

    def look(i):
        high, low = parts_of(i)
        ranks = dot(table[...], hot(high, highs), TN)
        picked = jnp.where(rows_of(ranks.shape) == low, ranks, 0.0)
        rank = jnp.sum(picked, axis=0, keepdims=True).astype(jnp.int32)
        name[:, window(i, nblock)] = lax.div(high, per) * CAP + rank

    looks = slots // nblock
    each(0, looks // 2, look)
    drain(wanted.at[0 : members - 1], all_recv.at[0])

    def feature_tile(index):
        return tile_of(
            features, lax.div(index, NEAR_FORWARD), width, lax.rem(index, NEAR_FORWARD), CAP
        )

    def feature_copy(k):
        return send_to(
            chosen.at[:, k * CAP : (k + 1) * CAP],
            feature_tile(me),
            all_send.at[1],
            all_recv.at[1],
            graph=peer_at(k),
        )

    some = members // TURNS
    for turn in range(TURNS):
        hot_of_ranks(wanted, hots, turn * some, (turn + 1) * some)
        lines = slice(turn * some * CAP, (turn + 1) * some * CAP)
        chosen[:, lines] = dot(feat, hots[lines, :], NT).astype(BF16)
        each(max(turn * some, 1), (turn + 1) * some, lambda k: feature_copy(k).start(), True)
    feature_tile(me)[...] = chosen[:, 0:CAP]
    each(looks // 2, looks, look)
    r["wbil"][...] = wbt_ref[...].astype(F32).T.astype(BF16)
    target = target_ref[...]
    atom_dev = atom_ref.shape[0]
    holder = lax.shift_right_logical(target, atom_dev.bit_length() - 1)
    line = lax.bitwise_and(holder, 1) * chips + lax.shift_right_logical(holder, 1)
    line = line * atom_dev + lax.bitwise_and(target, atom_dev - 1)
    line_hot, line_turn = r["line_hot"], r["line_turn"]
    lined = (rows_of((line_hot.shape[0], edges)) == line).astype(F32)
    line_hot[...] = lined.astype(BF16)
    line_turn[...] = lined.T.astype(BF16)
    drain(chosen.at[:, 0 : (members - 1) * CAP], all_recv.at[1])
    loads[0].wait()
    loads[1].wait()

    outgoing, basis_ref, total_ref = r["outgoing"], r["basis"], r["total"]
    spread = r["spread"]
    fblock = math.gcd(slots, BLOCK_FORWARD)
    far_shift = (NEAR_FORWARD * CAP).bit_length() - 1
    far = members // NEAR_FORWARD
    total_ref[...] = jnp.zeros_like(total_ref)

    def place_of(i, block):
        at = i * block + lax.broadcasted_iota(jnp.int32, (1, block), 1)
        return jnp.where(at < count_ref[0, 0], outgoing[:, window(i, block)], -1)

    def forward(i):
        here = window(i, fblock)
        index = name[:, here]
        group_of = lax.shift_right_logical(index, far_shift)
        all_wide = dot(features[...], hot(lax.bitwise_and(index, NEAR_FORWARD * CAP - 1), NEAR_FORWARD * CAP))
        feat = all_wide[0:width]
        for k in range(1, far):
            feat = jnp.where(group_of == k, all_wide[k * width : (k + 1) * width], feat)
        basis = basis_ref[:, here].astype(F32)
        for b in range(basis.shape[0]):
            spread[b * width : (b + 1) * width, :] = (basis[b : b + 1, :] * feat).astype(BF16)
        total_ref[...] += dot(spread[...], hot(place_of(i, fblock), edges), NT)

    each(0, slots // fblock, forward)

    parts, half, pair, arrived, grads, slope, gnew = (
        r["parts"], r["half"], r["pair"], r["arrived"], r["grads"], r["slope"], r["gnew"]
    )
    new_ref, anew_ref = r["new"], r["anew"]

    def leave(i):
        key = ("new", "anew", "gin", "wa_all", "wb_all", "wd_all")[i]
        return pltpu.make_async_copy(r[key], r[key + "_hbm"], load.at[4 + i])

    total = total_ref[...]
    high = total.astype(BF16)
    low = (total - high.astype(F32)).astype(BF16)
    gathered32 = dot(wbt_ref[...], high) + dot(wbt_ref[...], low)
    gathered = gathered32.astype(BF16)
    gathered_rows = gathered32.T.astype(BF16)
    part = wide // HALVES

    def pair_copy(q):
        rows = parts.shape[0] // 2
        lanes = slice(q * part, (q + 1) * part)
        return send_to(
            parts.at[pl.ds(pl.multiple_of(other * rows, rows), rows), lanes],
            half.at[:, lanes],
            all_send.at[2],
            many_recv.at[0, q],
            graph=partner,
        )

    for q in range(HALVES):
        lanes = slice(q * part, (q + 1) * part)
        update = dot(gathered_rows, wup_ref[:, lanes])
        new = (emb_ref[:, lanes].astype(F32) + silu(update)).astype(BF16)
        new_ref[:, lanes] = new
        slope[:, lanes] = silu_slope(update)
        parts[:, lanes] = dot(line_hot[...], new).astype(BF16)
        pair_copy(q).start()

    def chip_copy(k, lanes):
        c = chip_at(k)
        return send_to(
            some_rows(pair, c, atom_dev).at[:, lanes],
            arrived.at[chip, :, lanes],
            all_send.at[3],
            all_recv.at[3],
            graph=2 * c + core,
        )

    for q in range(HALVES):
        lanes = slice(q * part, (q + 1) * part)
        rows = parts.shape[0] // 2
        own = parts[pl.ds(pl.multiple_of(core * rows, rows), rows), lanes].astype(F32)
        pair_copy(q).wait_recv()
        pair[:, lanes] = (own + half[:, lanes].astype(F32)).astype(BF16)
        each(1, chips, lambda k: chip_copy(k, lanes).start(), True)
    arrived[chip] = some_rows(pair, chip, atom_dev)[...]
    loads[2].wait()
    loads[3].wait()
    watom_ref, gedge_ref = r["watom"], r["gedge"]
    drain(arrived.at[0 : chips - 1], all_recv.at[3])

    asum = jnp.sum(arrived[...].astype(F32), axis=0).astype(BF16)
    pre = ATOM_SCALE * dot(asum, watom_ref[...])
    grad_pre = (gatom_ref[...].astype(F32) * silu_slope(pre)).astype(BF16)
    some_rows(grads, mine(chip), atom_dev)[...] = (
        ATOM_SCALE * dot(grad_pre, watom_ref[...], NT)
    ).astype(BF16)

    def grad_copy(k):
        rows = some_rows(grads, mine(chip), atom_dev)
        return send_to(rows, rows, all_send.at[4], many_recv.at[1, k], graph=2 * chip_at(k) + core)

    def grad_pass(k):
        rows = some_rows(grads, mine(chip_from(k)), atom_dev)
        return send_to(rows, rows, all_send.at[5], all_recv.at[5], graph=partner)

    def grad_forward(k):
        grad_copy(k).wait_recv()
        grad_pass(k).start()

    each(1, chips, lambda k: grad_copy(k).start(), True)
    grad_pass(0).start()
    wa, wb = r["wa"], r["wb"]
    anew_ref[...] = (atom_ref[...].astype(F32) + silu(pre)).astype(BF16)
    wa[...] = (ATOM_SCALE * dot(asum, grad_pre, TN)).astype(BF16)
    leave(0).start()
    leave(1).start()
    each(1, chips, grad_forward, True)
    drain(half, all_recv.at[5])

    picked = dot(line_turn[...], grads[...])
    grad_new = gedge_ref[...].astype(F32) + picked
    gnew[...] = grad_new
    grad_update = (grad_new * slope[...]).astype(BF16)
    bil_wide = wbt_ref.shape[1]
    wb[:, bil_wide:] = dot(gathered, grad_update)
    gg = dot(wup_ref[...], grad_update, NT).astype(BF16)
    wb[:, :bil_wide] = dot(gg, total_ref[...].astype(BF16), NT)

    wa_half, wa_pair, wa_in, wa_dp, wa_all = r["wa_half"], r["wa_pair"], r["wa_in"], r["wa_dp"], r["wa_all"]
    wb_half, wb_pair, wb_in, wb_dp, wb_all = r["wb_half"], r["wb_pair"], r["wb_in"], r["wb_dp"], r["wb_all"]
    wa_rows = wa.shape[0] // members
    wb_rows = wb.shape[0] // 8
    wb_lanes = wb.shape[1] // SPLIT
    wb_split = chips // SPLIT

    def wb_tile(ref, c, base):
        return tile_of(ref, base * wb_split + lax.div(c, SPLIT), wb_rows, lax.rem(c, SPLIT), wb_lanes)

    def wa_duo():
        return send_to(
            some_rows(wa, other, wa.shape[0] // 2), wa_half, all_send.at[6], all_recv.at[6], graph=partner
        )

    def wb_duo():
        return send_to(
            some_rows(wb, other, wb.shape[0] // 2), wb_half, all_send.at[7], all_recv.at[7], graph=partner
        )

    def wa_far(k):
        c = chip_at(k)
        return send_to(
            some_rows(wa_pair, c, wa_rows), wa_in.at[chip], all_send.at[8], all_recv.at[8], graph=2 * c + core
        )

    def wb_far(k):
        c = chip_at(k)
        return send_to(
            wb_tile(wb_pair, c, 0), wb_in.at[chip], all_send.at[9], all_recv.at[9], graph=2 * c + core
        )

    def wa_group(k):
        return send_to(wa_dp.at[group], wa_dp.at[group], dp_send.at[0], dp_recv.at[0], dp=group_at(k))

    def wb_group(k):
        return send_to(wb_dp.at[group], wb_dp.at[group], dp_send.at[1], dp_recv.at[1], dp=group_at(k))

    def wa_back(k):
        rows = some_rows(wa_all, mine(chip), wa_rows)
        return send_to(rows, rows, all_send.at[10], all_recv.at[10], graph=2 * chip_at(k) + core)

    def wb_back(k):
        tile = wb_tile(wb_all, chip, core)
        return send_to(tile, tile, all_send.at[11], all_recv.at[11], graph=2 * chip_at(k) + core)

    def wa_pass():
        rows = some_rows(wa_all, core, wa.shape[0] // 2)
        return send_to(rows, rows, all_send.at[12], all_recv.at[12], graph=partner)

    def wb_pass():
        rows = some_rows(wb_all, core, wb.shape[0] // 2)
        return send_to(rows, rows, all_send.at[13], all_recv.at[13], graph=partner)

    def sums_pair():
        wa_duo().wait_recv()
        wb_duo().wait_recv()
        wa_pair[...] = (
            some_rows(wa, core, wa.shape[0] // 2)[...].astype(F32) + wa_half[...].astype(F32)
        ).astype(BF16)
        wb_pair[...] = some_rows(wb, core, wb.shape[0] // 2)[...] + wb_half[...]

    def sums_far():
        def go(k):
            wa_far(k).start()
            wb_far(k).start()

        each(1, chips, go, True)
        wa_in[chip] = some_rows(wa_pair, chip, wa_rows)[...]
        wb_in[chip] = wb_tile(wb_pair, chip, 0)[...]

    def sums_group():
        drain(wa_in.at[0 : chips - 1], all_recv.at[8])
        drain(wb_in.at[0 : chips - 1], all_recv.at[9])
        wa_dp[group] = jnp.sum(wa_in[...].astype(F32), axis=0)
        wb_dp[group] = jnp.sum(wb_in[...], axis=0)

        def go(k):
            wa_group(k).start()
            wb_group(k).start()

        each(1, groups, go, True)

    def sums_back():
        drain(wa_dp.at[0 : groups - 1], dp_recv.at[0])
        drain(wb_dp.at[0 : groups - 1], dp_recv.at[1])
        some_rows(wa_all, mine(chip), wa_rows)[...] = (scale * jnp.sum(wa_dp[...], axis=0)).astype(BF16)
        wb_tile(wb_all, chip, core)[...] = scale * jnp.sum(wb_dp[...], axis=0)

        def go(k):
            wa_back(k).start()
            wb_back(k).start()

        each(1, chips, go, True)

    def sums_pass():
        drain(wa_in.at[0 : chips - 1], all_recv.at[10])
        drain(wb_in.at[0 : chips - 1], all_recv.at[11])
        wa_pass().start()
        wb_pass().start()

    wa_duo().start()
    wb_duo().start()
    gg_two = r["gg_two"]
    gg_two[0:width, :] = gg[:, 0 : edges // 2]
    gg_two[width:, :] = gg[:, edges // 2 :]

    sent, back = r["sent"], r["back"]
    named, wbil = r["named"], r["wbil"]
    block = math.gcd(slots, BLOCK_BACKWARD)
    blocks = slots // block
    back_far = members // NEAR_BACKWARD
    back_shift = (NEAR_BACKWARD * CAP).bit_length() - 1
    named[...] = jnp.zeros_like(named)
    acts = {1: sums_pair, 2: sums_far, 8: sums_group, 10: sums_back, 14: sums_pass}
    masked = r["masked"]

    def backward(i):
        for at, act in acts.items():
            pl.when(i == at * blocks // 16)(act)
        here = window(i, block)
        place = place_of(i, block)
        both = dot(gg_two[...], hot(lax.bitwise_and(place, edges // 2 - 1), edges // 2))
        first = lax.shift_right_arithmetic(place, edges.bit_length() - 2)
        taken = jnp.where(first == 0, both[0:width], jnp.where(first == 1, both[width:], 0.0)).astype(BF16)
        backed = dot(wbil[...], taken)
        basis = basis_ref[:, here].astype(F32)
        grad = basis[0:1, :] * backed[0:width]
        for b in range(1, basis.shape[0]):
            grad = grad + basis[b : b + 1, :] * backed[b * width : (b + 1) * width]
        source = lax.shift_right_logical(name[:, here], back_shift)
        for k in range(back_far):
            masked[k * width : (k + 1) * width, :] = jnp.where(source == k, grad, 0.0).astype(BF16)
        near = lax.bitwise_and(name[:, window(i, block)], NEAR_BACKWARD * CAP - 1)
        named[...] += dot(masked[...], hot(near, NEAR_BACKWARD * CAP), NT)

    each(0, blocks, backward)

    sent[...] = named[...].astype(BF16)

    def sent_tile(index):
        return tile_of(sent, lax.div(index, NEAR_BACKWARD), width, lax.rem(index, NEAR_BACKWARD), CAP)

    def back_copy(k):
        peer = peer_at(k)
        there = members - k
        return send_to(
            sent_tile(peer),
            back.at[:, there * CAP : (there + 1) * CAP],
            all_send.at[14],
            all_recv.at[14],
            graph=peer,
        )

    each(1, members, lambda k: back_copy(k).start(), True)
    back[:, 0:CAP] = sent_tile(me)[...]
    wa_pass().wait_recv()
    wb_pass().wait_recv()
    leave(3).start()
    leave(4).start()
    drain(back.at[:, 0 : (members - 1) * CAP], all_recv.at[14])
    grad = dot(back[...], hots[...])
    grad = (grad * r["down_slope"][...]).astype(BF16)

    wd, wd_in, wd_dp, wd_all = r["wd"], r["wd_in"], r["wd_dp"], r["wd_all"]
    wd[...] = dot(grad, emb_ref[...])

    def wd_tile(ref, index):
        return tile_of(ref, lax.div(index, SPLIT), ref.shape[0] * SPLIT // members, lax.rem(index, SPLIT), LANES)

    def wd_far(k):
        peer = peer_at(k)
        return send_to(wd_tile(wd, peer), wd_in.at[me], all_send.at[15], all_recv.at[15], graph=peer)

    def wd_group(k):
        return send_to(wd_dp.at[group], wd_dp.at[group], dp_send.at[2], dp_recv.at[2], dp=group_at(k))

    def wd_back(k):
        tile = wd_tile(wd_all, me)
        return send_to(tile, tile, all_send.at[16], all_recv.at[16], graph=peer_at(k))

    each(1, members, lambda k: wd_far(k).start(), True)
    wd_in[me] = wd_tile(wd, me)[...]
    r["gin"][...] = gnew[...] + dot(grad, wdt_ref[...], TN)
    leave(2).start()
    drain(wd_in.at[0 : members - 1], all_recv.at[15])
    wd_dp[group] = jnp.sum(wd_in[...], axis=0)
    each(1, groups, lambda k: wd_group(k).start(), True)
    drain(wd_dp.at[0 : groups - 1], dp_recv.at[2])
    wd_tile(wd_all, me)[...] = scale * jnp.sum(wd_dp[...], axis=0)
    each(1, members, lambda k: wd_back(k).start(), True)

    drain(wanted.at[0 : members - 1], all_send.at[0])
    drain(chosen.at[:, 0 : (members - 1) * CAP], all_send.at[1])
    drain(half, all_send.at[2])
    drain(arrived.at[0 : chips - 1], all_send.at[3])
    drain(arrived.at[0 : chips - 1], all_send.at[4])
    drain(half, all_send.at[5])
    wa_duo().wait_send()
    wb_duo().wait_send()
    drain(wa_in.at[0 : chips - 1], all_send.at[8])
    drain(wb_in.at[0 : chips - 1], all_send.at[9])
    drain(wa_in.at[0 : chips - 1], all_send.at[10])
    drain(wb_in.at[0 : chips - 1], all_send.at[11])
    wa_pass().wait_send()
    wb_pass().wait_send()
    drain(wa_dp.at[0 : groups - 1], dp_send.at[0])
    drain(wb_dp.at[0 : groups - 1], dp_send.at[1])
    drain(wd_dp.at[0 : groups - 1], dp_send.at[2])
    drain(back.at[:, 0 : (members - 1) * CAP], all_send.at[14])
    drain(wd_in.at[0 : members - 1], all_send.at[15])
    drain(wd_in.at[0 : members - 1], all_send.at[16])
    drain(wd_in.at[0 : members - 1], all_recv.at[16])
    leave(5).start()
    for i in range(6):
        leave(i).wait()


def block_of(values, members, groups, scale):
    shape = jax.ShapeDtypeStruct
    edges, wide = values["emb"].shape
    atom_dev = values["atom"].shape[0]
    atoms = atom_dev * members
    width = values["wdt"].shape[0]
    slots = values["incoming"].shape[1]
    rows = values["wbt"].shape[1]
    chips = members // 2
    highs = members * edges // LANES
    per = highs // members
    all_wide = rows + wide
    piece = (width // 8, all_wide // SPLIT)
    wa_piece = (wide // members, wide)
    wd_piece = (width * SPLIT // members, wide // SPLIT)
    far = members // NEAR_FORWARD
    back_far = members // NEAR_BACKWARD
    late = ("outgoing", "basis", "watom", "gedge")
    ins, specs, args = [], [], []
    for key, value in values.items():
        if key in late:
            ins.append(key + "_hbm")
            specs.append(ANY)
        else:
            ins.append(key)
            specs.append(pl.BlockSpec(memory_space=pltpu.SMEM) if key == "count" else VMEM)
        args.append(value)
    outs = {
        "new": shape((edges, wide), BF16),
        "anew": shape((atom_dev, wide), BF16),
        "gin": shape((edges, wide), F32),
        "wa_all": shape((wide, wide), BF16),
        "wb_all": shape((width, all_wide), F32),
        "wd_all": shape((width, wide), F32),
    }
    scratch = {key: pltpu.VMEM(values[key].shape, values[key].dtype) for key in late}
    scratch |= {key: pltpu.VMEM(out.shape, out.dtype) for key, out in outs.items()}
    scratch |= {
        "table": pltpu.VMEM((highs, LANES), BF16),
        "found": pltpu.VMEM((highs, LANES), F32),
        "rank_buf": pltpu.VMEM((members, per, LANES), F32),
        "wanted": pltpu.VMEM((members, per, LANES), F32),
        "hots": pltpu.VMEM((members * CAP, edges), BF16),
        "chosen": pltpu.VMEM((width, members * CAP), BF16),
        "name": pltpu.VMEM((1, slots), jnp.int32),
        "features": pltpu.VMEM((far * width, NEAR_FORWARD * CAP), BF16),
        "down_slope": pltpu.VMEM((width, edges), F32),
        "wbil": pltpu.VMEM((rows, width), BF16),
        "spread": pltpu.VMEM((rows, math.gcd(slots, BLOCK_FORWARD)), BF16),
        "total": pltpu.VMEM((rows, edges), F32),
        "line_hot": pltpu.VMEM((atoms, edges), BF16),
        "line_turn": pltpu.VMEM((edges, atoms), BF16),
        "parts": pltpu.VMEM((atoms, wide), BF16),
        "half": pltpu.VMEM((atoms // 2, wide), BF16),
        "pair": pltpu.VMEM((atoms // 2, wide), BF16),
        "arrived": pltpu.VMEM((chips, atom_dev, wide), BF16),
        "grads": pltpu.VMEM((atoms, wide), BF16),
        "slope": pltpu.VMEM((edges, wide), F32),
        "gnew": pltpu.VMEM((edges, wide), F32),
        "wa": pltpu.VMEM((wide, wide), BF16),
        "wa_half": pltpu.VMEM((wide // 2, wide), BF16),
        "wa_pair": pltpu.VMEM((wide // 2, wide), BF16),
        "wa_in": pltpu.VMEM((chips, *wa_piece), BF16),
        "wa_dp": pltpu.VMEM((groups, *wa_piece), F32),
        "wb": pltpu.VMEM((width, all_wide), F32),
        "wb_half": pltpu.VMEM((width // 2, all_wide), F32),
        "wb_pair": pltpu.VMEM((width // 2, all_wide), F32),
        "wb_in": pltpu.VMEM((chips, *piece), F32),
        "wb_dp": pltpu.VMEM((groups, *piece), F32),
        "gg_two": pltpu.VMEM((2 * width, edges // 2), BF16),
        "named": pltpu.VMEM((back_far * width, NEAR_BACKWARD * CAP), F32),
        "masked": pltpu.VMEM((back_far * width, math.gcd(slots, BLOCK_BACKWARD)), BF16),
        "sent": pltpu.VMEM((back_far * width, NEAR_BACKWARD * CAP), BF16),
        "back": pltpu.VMEM((width, members * CAP), BF16),
        "wd": pltpu.VMEM((width, wide), F32),
        "wd_in": pltpu.VMEM((members, *wd_piece), F32),
        "wd_dp": pltpu.VMEM((groups, *wd_piece), F32),
        "all_send": pltpu.SemaphoreType.DMA((17,)),
        "all_recv": pltpu.SemaphoreType.DMA((17,)),
        "many_recv": pltpu.SemaphoreType.DMA((2, chips)),
        "dp_send": pltpu.SemaphoreType.DMA((3,)),
        "dp_recv": pltpu.SemaphoreType.DMA((3,)),
        "load": pltpu.SemaphoreType.DMA((10,)),
    }
    return pl.pallas_call(
        functools.partial(block_kernel, members, groups, scale, (*ins, *(key + "_hbm" for key in outs), *scratch)),
        out_shape=tuple(outs.values()),
        in_specs=specs,
        out_specs=(ANY,) * len(outs),
        scratch_shapes=list(scratch.values()),
        compiler_params=params(collective_id=1, has_side_effects=True),
        name="block",
    )(*args)


def finish_kernel(*refs):
    ins, outs, bufs, (wide_buf, got, put) = refs[:6], refs[6:13], refs[13:19], refs[19:]
    new, anew, gin, wa, wb, wd = bufs
    takes = [pltpu.make_async_copy(ins[i], bufs[i], got.at[i]) for i in range(6)]
    order = (3, 2, 0, 4, 5, 1)
    for i in order:
        takes[i].start()
    bil_wide = outs[4].shape[1]
    gives = {
        3: [(wide_buf, outs[6])],
        2: [(gin, outs[2])],
        0: [(new, outs[0])],
        4: [(wb.at[:, 0:bil_wide], outs[4]), (wb.at[:, bil_wide:], outs[5])],
        5: [(wd, outs[3])],
        1: [(anew, outs[1])],
    }
    started = []
    for i in order:
        takes[i].wait()
        if i == 3:
            wide_buf[...] = wa[...].astype(F32)
        for src, dst in gives[i]:
            one = pltpu.make_async_copy(src, dst, put.at[len(started)])
            one.start()
            started.append(one)
    for one in started:
        one.wait()


def finish(new, anew, gin, wa, wb, wd):
    shape = jax.ShapeDtypeStruct
    wide = wa.shape[1]
    width = wb.shape[0]
    ins = (new, anew, gin, wa, wb, wd)
    return pl.pallas_call(
        finish_kernel,
        out_shape=(
            shape(new.shape, BF16),
            shape(anew.shape, BF16),
            shape(gin.shape, F32),
            shape(wd.shape, F32),
            shape((width, wb.shape[1] - wide), F32),
            shape((width, wide), F32),
            shape(wa.shape, F32),
        ),
        in_specs=[ANY] * 6,
        out_specs=(ANY,) * 7,
        scratch_shapes=[pltpu.VMEM(one.shape, one.dtype) for one in ins]
        + [pltpu.VMEM(wa.shape, F32), pltpu.SemaphoreType.DMA((6,)), pltpu.SemaphoreType.DMA((7,))],
        compiler_params=params(),
        name="finish",
    )(*ins)


def body(
    groups,
    members,
    edge_emb,
    atom_emb,
    edge_target,
    trip_in,
    trip_out,
    trip_count,
    trip_basis,
    grad_edge,
    grad_atom,
    w_down,
    w_bil,
    w_up,
    w_atom,
):
    scale = 1.0 / math.sqrt(groups * members * edge_emb.shape[1])
    values = dict(
        incoming=trip_in,
        emb=edge_emb[0],
        wdt=w_down.T,
        wbt=w_bil.T,
        wup=w_up,
        target=edge_target,
        atom=atom_emb[0],
        gatom=grad_atom[0],
        count=trip_count,
        outgoing=trip_out,
        basis=trip_basis[0],
        watom=w_atom,
        gedge=grad_edge[0],
    )
    edge_new, atom_new, grad_in, down, bil, up, atom = finish(*block_of(values, members, groups, scale))
    return (edge_new[None], atom_new[None], grad_in[None], down.T, bil.T, up, atom)


def solution(mesh):
    graph = P("dp", "graph")
    rows = P("dp", "graph", None)
    return jax.shard_map(
        functools.partial(body, mesh.shape["dp"], mesh.shape["graph"]),
        mesh=mesh,
        in_specs=(rows, rows, graph, graph, graph, graph, P("dp", None, "graph"), rows, rows)
        + (P(),) * 4,
        out_specs=(rows, rows, rows) + (P(),) * 4,
        check_vma=False,
    )
```

```python
import functools
import math

import jax
import jax.numpy as jnp
from jax import lax
from jax.experimental import pallas as pl
from jax.experimental.pallas import tpu as pltpu
from jax.sharding import PartitionSpec as P

MESH = pl.DeviceIdType.MESH
F32 = jnp.float32
HALVES = 2
TURNS = 4
BF16 = jnp.bfloat16
ATOM_SCALE = 0.25
CAP = 128
LANES = 128
NEAR_FORWARD = 2
NEAR_BACKWARD = 4
SPLIT = 4
BLOCK_NAMES = 4096
BLOCK_FORWARD = 2048
BLOCK_BACKWARD = 2048
ANY = pl.BlockSpec(memory_space=pl.ANY)
VMEM = pl.BlockSpec(memory_space=pltpu.VMEM)
NN = (((1,), (0,)), ((), ()))
NT = (((1,), (1,)), ((), ()))
TN = (((0,), (0,)), ((), ()))


def dot(a, b, dims=NN):
    return lax.dot_general(a, b, dims, preferred_element_type=F32)


def rows_of(shape):
    return lax.broadcasted_iota(jnp.int32, shape, 0)


def hot(index, size):
    return (rows_of((size, index.shape[1])) == index).astype(F32).astype(BF16)


def silu_slope(value):
    logistic = jax.nn.sigmoid(value)
    return logistic * (1.0 + value * (1.0 - logistic))


def silu(value):
    return value * jax.nn.sigmoid(value)


def params(**kw):
    return pltpu.CompilerParams(vmem_limit_bytes=60 * 1024 * 1024, **kw)


def send_to(src, dst, send, recv, **where):
    return pltpu.make_async_remote_copy(
        src_ref=src,
        dst_ref=dst,
        send_sem=send,
        recv_sem=recv,
        device_id=where,
        device_id_type=MESH,
    )


def drain(ref, sem):
    pltpu.make_async_copy(ref, ref, sem).wait()


def each(first, last, act, unroll=False):
    if unroll:
        for k in range(first, last):
            act(k)
        return

    def one(k, c):
        act(k)
        return c

    lax.fori_loop(first, last, one, 0)


def wrap(value, size):
    return jnp.where(value >= size, value - size, value)


def some_rows(ref, index, rows):
    return ref.at[pl.ds(pl.multiple_of(index * rows, rows), rows), :]


def tile_of(ref, row, rows, lane, lanes):
    return ref.at[
        pl.ds(pl.multiple_of(row * rows, rows), rows),
        pl.ds(pl.multiple_of(lane * lanes, lanes), lanes),
    ]


def hot_of_ranks(rank_ref, hot_ref, first, last):
    per = rank_ref.shape[1]
    place = lax.broadcasted_iota(jnp.int32, (CAP, LANES), 0).astype(F32)

    def one(d):
        ranks = rank_ref[d]
        at = pl.ds(pl.multiple_of(d * CAP, CAP), CAP)
        for q in range(per):
            hot_ref[at, q * LANES : (q + 1) * LANES] = (
                (place == ranks[q : q + 1, :]).astype(F32).astype(BF16)
            )

    each(first, last, one)


def block_kernel(members, groups, scale, names_of, *refs):
    r = dict(zip(names_of, refs))
    (in_ref, emb_ref, wdt_ref, wbt_ref, wup_ref, target_ref, atom_ref, gatom_ref, count_ref) = (
        r["incoming"], r["emb"], r["wdt"], r["wbt"], r["wup"], r["target"], r["atom"], r["gatom"], r["count"]
    )
    me = lax.axis_index("graph")
    group = lax.axis_index("dp")
    chips = members // 2
    chip = lax.div(me, 2)
    core = lax.rem(me, 2)
    other = 1 - core
    partner = 2 * chip + other
    all_send, all_recv, many_recv, dp_send, dp_recv, load = (
        r["all_send"], r["all_recv"], r["many_recv"], r["dp_send"], r["dp_recv"], r["load"]
    )

    def peer_at(k):
        return wrap(me + k, members)

    def chip_at(k):
        return wrap(chip + k, chips)

    def chip_from(k):
        return wrap(chip + chips - k, chips)

    def group_at(k):
        return wrap(group + k, groups)

    def mine(c):
        return core * chips + c

    loads = [
        pltpu.make_async_copy(r[name + "_hbm"], r[name], load.at[i])
        for i, name in enumerate(("outgoing", "basis", "watom", "gedge"))
    ]
    for one in loads:
        one.start()
    barrier = pltpu.get_barrier_semaphore()
    each(
        1,
        members,
        lambda k: pl.semaphore_signal(
            barrier, inc=1, device_id={"graph": peer_at(k)}, device_id_type=MESH
        ),
        True,
    )
    each(
        1,
        groups,
        lambda k: pl.semaphore_signal(
            barrier, inc=1, device_id={"dp": group_at(k)}, device_id_type=MESH
        ),
        True,
    )

    table, found, rank_buf, wanted, hots, chosen, name, features = (
        r["table"], r["found"], r["rank_buf"], r["wanted"], r["hots"], r["chosen"], r["name"], r["features"]
    )
    highs = table.shape[0]
    per = highs // members
    width = wdt_ref.shape[0]
    edges, wide = emb_ref.shape
    slots = in_ref.shape[1]
    nblock = math.gcd(slots, BLOCK_NAMES)

    def window(i, block):
        return pl.ds(pl.multiple_of(i * block, block), block)

    def parts_of(i):
        index = in_ref[:, window(i, nblock)]
        return lax.shift_right_logical(index, 7), lax.bitwise_and(index, LANES - 1)

    found[...] = jnp.zeros_like(found)

    def find(i):
        high, low = parts_of(i)
        found[...] += dot(hot(high, highs), hot(low, LANES), NT)

    each(0, slots // nblock, find)
    there = jnp.where(found[...] > 0.0, 1.0, 0.0)
    there16 = there.astype(BF16)
    row = lax.broadcasted_iota(jnp.int32, (LANES, LANES), 0)
    col = lax.broadcasted_iota(jnp.int32, (LANES, LANES), 1)
    upper = (row <= col).astype(F32).astype(BF16)
    hrow = lax.broadcasted_iota(jnp.int32, (highs, highs), 0)
    hcol = lax.broadcasted_iota(jnp.int32, (highs, highs), 1)
    before = ((hcol < hrow) & (lax.div(hcol, per) == lax.div(hrow, per))).astype(F32).astype(BF16)
    ahead = dot(before, there16).astype(BF16)
    ones = jnp.ones((LANES, LANES), BF16)
    rank = dot(there16, upper) + dot(ahead, ones) - 1.0
    rank = jnp.where(there > 0.0, rank, -1.0)
    table[...] = rank.astype(BF16)
    for s in range(members):
        rank_buf[s] = rank[s * per : (s + 1) * per, :]
    proj = dot(wdt_ref[...], emb_ref[...], NT)
    feat = silu(proj).astype(BF16)
    r["down_slope"][...] = silu_slope(proj)
    pl.semaphore_wait(barrier, members - 1 + groups - 1)

    def rank_copy(k):
        peer = peer_at(k)
        return send_to(
            rank_buf.at[peer], wanted.at[members - k], all_send.at[0], all_recv.at[0], graph=peer
        )

    each(1, members, lambda k: rank_copy(k).start(), True)
    wanted[0] = rank_buf[me]

    def look(i):
        high, low = parts_of(i)
        ranks = dot(table[...], hot(high, highs), TN)
        picked = jnp.where(rows_of(ranks.shape) == low, ranks, 0.0)
        rank = jnp.sum(picked, axis=0, keepdims=True).astype(jnp.int32)
        name[:, window(i, nblock)] = lax.div(high, per) * CAP + rank

    looks = slots // nblock
    each(0, looks // 2, look)
    drain(wanted.at[0 : members - 1], all_recv.at[0])

    def feature_tile(index):
        return tile_of(
            features, lax.div(index, NEAR_FORWARD), width, lax.rem(index, NEAR_FORWARD), CAP
        )

    def feature_copy(k):
        return send_to(
            chosen.at[:, k * CAP : (k + 1) * CAP],
            feature_tile(me),
            all_send.at[1],
            all_recv.at[1],
            graph=peer_at(k),
        )

    some = members // TURNS
    for turn in range(TURNS):
        hot_of_ranks(wanted, hots, turn * some, (turn + 1) * some)
        lines = slice(turn * some * CAP, (turn + 1) * some * CAP)
        chosen[:, lines] = dot(feat, hots[lines, :], NT).astype(BF16)
        each(max(turn * some, 1), (turn + 1) * some, lambda k: feature_copy(k).start(), True)
    feature_tile(me)[...] = chosen[:, 0:CAP]
    each(looks // 2, looks, look)
    r["wbil"][...] = wbt_ref[...].astype(F32).T.astype(BF16)
    target = target_ref[...]
    atom_dev = atom_ref.shape[0]
    holder = lax.shift_right_logical(target, atom_dev.bit_length() - 1)
    line = lax.bitwise_and(holder, 1) * chips + lax.shift_right_logical(holder, 1)
    line = line * atom_dev + lax.bitwise_and(target, atom_dev - 1)
    line_hot, line_turn = r["line_hot"], r["line_turn"]
    lined = (rows_of((line_hot.shape[0], edges)) == line).astype(F32)
    line_hot[...] = lined.astype(BF16)
    line_turn[...] = lined.T.astype(BF16)
    drain(chosen.at[:, 0 : (members - 1) * CAP], all_recv.at[1])
    loads[0].wait()
    loads[1].wait()

    outgoing, basis_ref, total_ref = r["outgoing"], r["basis"], r["total"]
    spread = r["spread"]
    fblock = math.gcd(slots, BLOCK_FORWARD)
    far_shift = (NEAR_FORWARD * CAP).bit_length() - 1
    far = members // NEAR_FORWARD
    total_ref[...] = jnp.zeros_like(total_ref)

    def place_of(i, block):
        at = i * block + lax.broadcasted_iota(jnp.int32, (1, block), 1)
        return jnp.where(at < count_ref[0, 0], outgoing[:, window(i, block)], -1)

    def forward(i):
        here = window(i, fblock)
        index = name[:, here]
        group_of = lax.shift_right_logical(index, far_shift)
        all_wide = dot(features[...], hot(lax.bitwise_and(index, NEAR_FORWARD * CAP - 1), NEAR_FORWARD * CAP))
        feat = all_wide[0:width]
        for k in range(1, far):
            feat = jnp.where(group_of == k, all_wide[k * width : (k + 1) * width], feat)
        basis = basis_ref[:, here].astype(F32)
        for b in range(basis.shape[0]):
            spread[b * width : (b + 1) * width, :] = (basis[b : b + 1, :] * feat).astype(BF16)
        total_ref[...] += dot(spread[...], hot(place_of(i, fblock), edges), NT)

    each(0, slots // fblock, forward)

    parts, half, pair, arrived, grads, slope, gnew = (
        r["parts"], r["half"], r["pair"], r["arrived"], r["grads"], r["slope"], r["gnew"]
    )
    new_ref, anew_ref = r["new"], r["anew"]

    def leave(i):
        key = ("new", "anew", "gin", "wa_all", "wb_all", "wd_all")[i]
        return pltpu.make_async_copy(r[key], r[key + "_hbm"], load.at[4 + i])

    total = total_ref[...]
    high = total.astype(BF16)
    low = (total - high.astype(F32)).astype(BF16)
    gathered32 = dot(wbt_ref[...], high) + dot(wbt_ref[...], low)
    gathered = gathered32.astype(BF16)
    gathered_rows = gathered32.T.astype(BF16)
    part = wide // HALVES

    def pair_copy(q):
        rows = parts.shape[0] // 2
        lanes = slice(q * part, (q + 1) * part)
        return send_to(
            parts.at[pl.ds(pl.multiple_of(other * rows, rows), rows), lanes],
            half.at[:, lanes],
            all_send.at[2],
            many_recv.at[0, q],
            graph=partner,
        )

    for q in range(HALVES):
        lanes = slice(q * part, (q + 1) * part)
        update = dot(gathered_rows, wup_ref[:, lanes])
        new = (emb_ref[:, lanes].astype(F32) + silu(update)).astype(BF16)
        new_ref[:, lanes] = new
        slope[:, lanes] = update
        parts[:, lanes] = dot(line_hot[...], new).astype(BF16)
        pair_copy(q).start()

    def chip_copy(k, lanes):
        c = chip_at(k)
        return send_to(
            some_rows(pair, c, atom_dev).at[:, lanes],
            arrived.at[chip, :, lanes],
            all_send.at[3],
            all_recv.at[3],
            graph=2 * c + core,
        )

    for q in range(HALVES):
        lanes = slice(q * part, (q + 1) * part)
        rows = parts.shape[0] // 2
        own = parts[pl.ds(pl.multiple_of(core * rows, rows), rows), lanes].astype(F32)
        pair_copy(q).wait_recv()
        pair[:, lanes] = (own + half[:, lanes].astype(F32)).astype(BF16)
        each(1, chips, lambda k: chip_copy(k, lanes).start(), True)
    arrived[chip] = some_rows(pair, chip, atom_dev)[...]
    slope[...] = silu_slope(slope[...])
    loads[2].wait()
    loads[3].wait()
    watom_ref, gedge_ref = r["watom"], r["gedge"]
    drain(arrived.at[0 : chips - 1], all_recv.at[3])

    asum = jnp.sum(arrived[...].astype(F32), axis=0).astype(BF16)
    pre = ATOM_SCALE * dot(asum, watom_ref[...])
    grad_pre = (gatom_ref[...].astype(F32) * silu_slope(pre)).astype(BF16)
    some_rows(grads, mine(chip), atom_dev)[...] = (
        ATOM_SCALE * dot(grad_pre, watom_ref[...], NT)
    ).astype(BF16)

    def grad_copy(k):
        rows = some_rows(grads, mine(chip), atom_dev)
        return send_to(rows, rows, all_send.at[4], many_recv.at[1, k], graph=2 * chip_at(k) + core)

    def grad_pass(k):
        rows = some_rows(grads, mine(chip_from(k)), atom_dev)
        return send_to(rows, rows, all_send.at[5], all_recv.at[5], graph=partner)

    def grad_forward(k):
        grad_copy(k).wait_recv()
        grad_pass(k).start()

    each(1, chips, lambda k: grad_copy(k).start(), True)
    grad_pass(0).start()
    wa, wb = r["wa"], r["wb"]
    anew_ref[...] = (atom_ref[...].astype(F32) + silu(pre)).astype(BF16)
    wa[...] = (ATOM_SCALE * dot(asum, grad_pre, TN)).astype(BF16)
    def wa_duo():
        return send_to(
            some_rows(wa, other, wa.shape[0] // 2), r["wa_half"], all_send.at[6], all_recv.at[6], graph=partner
        )

    leave(0).start()
    leave(1).start()
    each(1, chips, grad_forward, True)
    wa_duo().start()
    drain(half, all_recv.at[5])

    picked = dot(line_turn[...], grads[...])
    grad_new = gedge_ref[...].astype(F32) + picked
    gnew[...] = grad_new
    grad_update = (grad_new * slope[...]).astype(BF16)
    bil_wide = wbt_ref.shape[1]
    wb[:, bil_wide:] = dot(gathered, grad_update)
    gg = dot(wup_ref[...], grad_update, NT).astype(BF16)
    wb[:, :bil_wide] = dot(gg, total_ref[...].astype(BF16), NT)

    wa_half, wa_pair, wa_in, wa_dp, wa_all = r["wa_half"], r["wa_pair"], r["wa_in"], r["wa_dp"], r["wa_all"]
    wb_half, wb_pair, wb_in, wb_dp, wb_all = r["wb_half"], r["wb_pair"], r["wb_in"], r["wb_dp"], r["wb_all"]
    wa_rows = wa.shape[0] // members
    wb_rows = wb.shape[0] // 8
    wb_lanes = wb.shape[1] // SPLIT
    wb_split = chips // SPLIT

    def wb_tile(ref, c, base):
        return tile_of(ref, base * wb_split + lax.div(c, SPLIT), wb_rows, lax.rem(c, SPLIT), wb_lanes)

    def wb_duo():
        return send_to(
            some_rows(wb, other, wb.shape[0] // 2), wb_half, all_send.at[7], all_recv.at[7], graph=partner
        )

    def wa_far(k):
        c = chip_at(k)
        return send_to(
            some_rows(wa_pair, c, wa_rows), wa_in.at[chip], all_send.at[8], all_recv.at[8], graph=2 * c + core
        )

    def wb_far(k):
        c = chip_at(k)
        return send_to(
            wb_tile(wb_pair, c, 0), wb_in.at[chip], all_send.at[9], all_recv.at[9], graph=2 * c + core
        )

    def wa_group(k):
        return send_to(wa_dp.at[group], wa_dp.at[group], dp_send.at[0], dp_recv.at[0], dp=group_at(k))

    def wb_group(k):
        return send_to(wb_dp.at[group], wb_dp.at[group], dp_send.at[1], dp_recv.at[1], dp=group_at(k))

    def wa_back(k):
        rows = some_rows(wa_all, mine(chip), wa_rows)
        return send_to(rows, rows, all_send.at[10], all_recv.at[10], graph=2 * chip_at(k) + core)

    def wb_back(k):
        tile = wb_tile(wb_all, chip, core)
        return send_to(tile, tile, all_send.at[11], all_recv.at[11], graph=2 * chip_at(k) + core)

    def wa_pass():
        rows = some_rows(wa_all, core, wa.shape[0] // 2)
        return send_to(rows, rows, all_send.at[12], all_recv.at[12], graph=partner)

    def wb_pass():
        rows = some_rows(wb_all, core, wb.shape[0] // 2)
        return send_to(rows, rows, all_send.at[13], all_recv.at[13], graph=partner)

    def sums_pair():
        wa_duo().wait_recv()
        wb_duo().wait_recv()
        wa_pair[...] = (
            some_rows(wa, core, wa.shape[0] // 2)[...].astype(F32) + wa_half[...].astype(F32)
        ).astype(BF16)
        wb_pair[...] = some_rows(wb, core, wb.shape[0] // 2)[...] + wb_half[...]

    def sums_far():
        def go(k):
            wa_far(k).start()
            wb_far(k).start()

        each(1, chips, go, True)
        wa_in[chip] = some_rows(wa_pair, chip, wa_rows)[...]
        wb_in[chip] = wb_tile(wb_pair, chip, 0)[...]

    def sums_group():
        drain(wa_in.at[0 : chips - 1], all_recv.at[8])
        drain(wb_in.at[0 : chips - 1], all_recv.at[9])
        wa_dp[group] = jnp.sum(wa_in[...].astype(F32), axis=0)
        wb_dp[group] = jnp.sum(wb_in[...], axis=0)

        def go(k):
            wa_group(k).start()
            wb_group(k).start()

        each(1, groups, go, True)

    def sums_back():
        drain(wa_dp.at[0 : groups - 1], dp_recv.at[0])
        drain(wb_dp.at[0 : groups - 1], dp_recv.at[1])
        some_rows(wa_all, mine(chip), wa_rows)[...] = (scale * jnp.sum(wa_dp[...], axis=0)).astype(BF16)
        wb_tile(wb_all, chip, core)[...] = scale * jnp.sum(wb_dp[...], axis=0)

        def go(k):
            wa_back(k).start()
            wb_back(k).start()

        each(1, chips, go, True)

    def sums_pass():
        drain(wa_in.at[0 : chips - 1], all_recv.at[10])
        drain(wb_in.at[0 : chips - 1], all_recv.at[11])
        wa_pass().start()
        wb_pass().start()

    wb_duo().start()
    gg_two = r["gg_two"]
    gg_two[0:width, :] = gg[:, 0 : edges // 2]
    gg_two[width:, :] = gg[:, edges // 2 :]

    sent, back = r["sent"], r["back"]
    named, wbil = r["named"], r["wbil"]
    block = math.gcd(slots, BLOCK_BACKWARD)
    blocks = slots // block
    back_far = members // NEAR_BACKWARD
    back_shift = (NEAR_BACKWARD * CAP).bit_length() - 1
    named[...] = jnp.zeros_like(named)
    acts = {1: sums_pair, 2: sums_far, 9: sums_group, 11: sums_back}
    masked = r["masked"]

    def backward(i):
        for at, act in acts.items():
            pl.when(i == at * blocks // 16)(act)
        here = window(i, block)
        place = place_of(i, block)
        both = dot(gg_two[...], hot(lax.bitwise_and(place, edges // 2 - 1), edges // 2))
        first = lax.shift_right_arithmetic(place, edges.bit_length() - 2)
        taken = jnp.where(first == 0, both[0:width], jnp.where(first == 1, both[width:], 0.0)).astype(BF16)
        backed = dot(wbil[...], taken)
        basis = basis_ref[:, here].astype(F32)
        grad = basis[0:1, :] * backed[0:width]
        for b in range(1, basis.shape[0]):
            grad = grad + basis[b : b + 1, :] * backed[b * width : (b + 1) * width]
        source = lax.shift_right_logical(name[:, here], back_shift)
        for k in range(back_far):
            masked[k * width : (k + 1) * width, :] = jnp.where(source == k, grad, 0.0).astype(BF16)
        near = lax.bitwise_and(name[:, window(i, block)], NEAR_BACKWARD * CAP - 1)
        named[...] += dot(masked[...], hot(near, NEAR_BACKWARD * CAP), NT)

    each(0, blocks, backward)

    sent[...] = named[...].astype(BF16)

    def sent_tile(index):
        return tile_of(sent, lax.div(index, NEAR_BACKWARD), width, lax.rem(index, NEAR_BACKWARD), CAP)

    def back_copy(k):
        peer = peer_at(k)
        there = members - k
        return send_to(
            sent_tile(peer),
            back.at[:, there * CAP : (there + 1) * CAP],
            all_send.at[14],
            all_recv.at[14],
            graph=peer,
        )

    each(1, members, lambda k: back_copy(k).start(), True)
    back[:, 0:CAP] = sent_tile(me)[...]
    sums_pass()
    wa_pass().wait_recv()
    wb_pass().wait_recv()
    leave(3).start()
    leave(4).start()
    drain(back.at[:, 0 : (members - 1) * CAP], all_recv.at[14])
    grad = dot(back[...], hots[...])
    grad = (grad * r["down_slope"][...]).astype(BF16)

    wd, wd_in, wd_dp, wd_all = r["wd"], r["wd_in"], r["wd_dp"], r["wd_all"]
    wd[...] = dot(grad, emb_ref[...])

    def wd_tile(ref, index):
        return tile_of(ref, lax.div(index, SPLIT), ref.shape[0] * SPLIT // members, lax.rem(index, SPLIT), LANES)

    def wd_far(k):
        peer = peer_at(k)
        return send_to(wd_tile(wd, peer), wd_in.at[me], all_send.at[15], all_recv.at[15], graph=peer)

    def wd_group(k):
        return send_to(wd_dp.at[group], wd_dp.at[group], dp_send.at[2], dp_recv.at[2], dp=group_at(k))

    def wd_back(k):
        tile = wd_tile(wd_all, me)
        return send_to(tile, tile, all_send.at[16], all_recv.at[16], graph=peer_at(k))

    each(1, members, lambda k: wd_far(k).start(), True)
    wd_in[me] = wd_tile(wd, me)[...]
    r["gin"][...] = gnew[...] + dot(grad, wdt_ref[...], TN)
    leave(2).start()
    drain(wd_in.at[0 : members - 1], all_recv.at[15])
    wd_dp[group] = jnp.sum(wd_in[...], axis=0)
    each(1, groups, lambda k: wd_group(k).start(), True)
    drain(wd_dp.at[0 : groups - 1], dp_recv.at[2])
    wd_tile(wd_all, me)[...] = scale * jnp.sum(wd_dp[...], axis=0)
    each(1, members, lambda k: wd_back(k).start(), True)

    drain(wanted.at[0 : members - 1], all_send.at[0])
    drain(chosen.at[:, 0 : (members - 1) * CAP], all_send.at[1])
    drain(half, all_send.at[2])
    drain(arrived.at[0 : chips - 1], all_send.at[3])
    drain(arrived.at[0 : chips - 1], all_send.at[4])
    drain(half, all_send.at[5])
    wa_duo().wait_send()
    wb_duo().wait_send()
    drain(wa_in.at[0 : chips - 1], all_send.at[8])
    drain(wb_in.at[0 : chips - 1], all_send.at[9])
    drain(wa_in.at[0 : chips - 1], all_send.at[10])
    drain(wb_in.at[0 : chips - 1], all_send.at[11])
    wa_pass().wait_send()
    wb_pass().wait_send()
    drain(wa_dp.at[0 : groups - 1], dp_send.at[0])
    drain(wb_dp.at[0 : groups - 1], dp_send.at[1])
    drain(wd_dp.at[0 : groups - 1], dp_send.at[2])
    drain(back.at[:, 0 : (members - 1) * CAP], all_send.at[14])
    drain(wd_in.at[0 : members - 1], all_send.at[15])
    drain(wd_in.at[0 : members - 1], all_send.at[16])
    drain(wd_in.at[0 : members - 1], all_recv.at[16])
    leave(5).start()
    for i in range(6):
        leave(i).wait()


def block_of(values, members, groups, scale):
    shape = jax.ShapeDtypeStruct
    edges, wide = values["emb"].shape
    atom_dev = values["atom"].shape[0]
    atoms = atom_dev * members
    width = values["wdt"].shape[0]
    slots = values["incoming"].shape[1]
    rows = values["wbt"].shape[1]
    chips = members // 2
    highs = members * edges // LANES
    per = highs // members
    all_wide = rows + wide
    piece = (width // 8, all_wide // SPLIT)
    wa_piece = (wide // members, wide)
    wd_piece = (width * SPLIT // members, wide // SPLIT)
    far = members // NEAR_FORWARD
    back_far = members // NEAR_BACKWARD
    late = ("outgoing", "basis", "watom", "gedge")
    ins, specs, args = [], [], []
    for key, value in values.items():
        if key in late:
            ins.append(key + "_hbm")
            specs.append(ANY)
        else:
            ins.append(key)
            specs.append(pl.BlockSpec(memory_space=pltpu.SMEM) if key == "count" else VMEM)
        args.append(value)
    outs = {
        "new": shape((edges, wide), BF16),
        "anew": shape((atom_dev, wide), BF16),
        "gin": shape((edges, wide), F32),
        "wa_all": shape((wide, wide), BF16),
        "wb_all": shape((width, all_wide), F32),
        "wd_all": shape((width, wide), F32),
    }
    scratch = {key: pltpu.VMEM(values[key].shape, values[key].dtype) for key in late}
    scratch |= {key: pltpu.VMEM(out.shape, out.dtype) for key, out in outs.items()}
    scratch |= {
        "table": pltpu.VMEM((highs, LANES), BF16),
        "found": pltpu.VMEM((highs, LANES), F32),
        "rank_buf": pltpu.VMEM((members, per, LANES), F32),
        "wanted": pltpu.VMEM((members, per, LANES), F32),
        "hots": pltpu.VMEM((members * CAP, edges), BF16),
        "chosen": pltpu.VMEM((width, members * CAP), BF16),
        "name": pltpu.VMEM((1, slots), jnp.int32),
        "features": pltpu.VMEM((far * width, NEAR_FORWARD * CAP), BF16),
        "down_slope": pltpu.VMEM((width, edges), F32),
        "wbil": pltpu.VMEM((rows, width), BF16),
        "spread": pltpu.VMEM((rows, math.gcd(slots, BLOCK_FORWARD)), BF16),
        "total": pltpu.VMEM((rows, edges), F32),
        "line_hot": pltpu.VMEM((atoms, edges), BF16),
        "line_turn": pltpu.VMEM((edges, atoms), BF16),
        "parts": pltpu.VMEM((atoms, wide), BF16),
        "half": pltpu.VMEM((atoms // 2, wide), BF16),
        "pair": pltpu.VMEM((atoms // 2, wide), BF16),
        "arrived": pltpu.VMEM((chips, atom_dev, wide), BF16),
        "grads": pltpu.VMEM((atoms, wide), BF16),
        "slope": pltpu.VMEM((edges, wide), F32),
        "gnew": pltpu.VMEM((edges, wide), F32),
        "wa": pltpu.VMEM((wide, wide), BF16),
        "wa_half": pltpu.VMEM((wide // 2, wide), BF16),
        "wa_pair": pltpu.VMEM((wide // 2, wide), BF16),
        "wa_in": pltpu.VMEM((chips, *wa_piece), BF16),
        "wa_dp": pltpu.VMEM((groups, *wa_piece), F32),
        "wb": pltpu.VMEM((width, all_wide), F32),
        "wb_half": pltpu.VMEM((width // 2, all_wide), F32),
        "wb_pair": pltpu.VMEM((width // 2, all_wide), F32),
        "wb_in": pltpu.VMEM((chips, *piece), F32),
        "wb_dp": pltpu.VMEM((groups, *piece), F32),
        "gg_two": pltpu.VMEM((2 * width, edges // 2), BF16),
        "named": pltpu.VMEM((back_far * width, NEAR_BACKWARD * CAP), F32),
        "masked": pltpu.VMEM((back_far * width, math.gcd(slots, BLOCK_BACKWARD)), BF16),
        "sent": pltpu.VMEM((back_far * width, NEAR_BACKWARD * CAP), BF16),
        "back": pltpu.VMEM((width, members * CAP), BF16),
        "wd": pltpu.VMEM((width, wide), F32),
        "wd_in": pltpu.VMEM((members, *wd_piece), F32),
        "wd_dp": pltpu.VMEM((groups, *wd_piece), F32),
        "all_send": pltpu.SemaphoreType.DMA((17,)),
        "all_recv": pltpu.SemaphoreType.DMA((17,)),
        "many_recv": pltpu.SemaphoreType.DMA((2, chips)),
        "dp_send": pltpu.SemaphoreType.DMA((3,)),
        "dp_recv": pltpu.SemaphoreType.DMA((3,)),
        "load": pltpu.SemaphoreType.DMA((10,)),
    }
    return pl.pallas_call(
        functools.partial(block_kernel, members, groups, scale, (*ins, *(key + "_hbm" for key in outs), *scratch)),
        out_shape=tuple(outs.values()),
        in_specs=specs,
        out_specs=(ANY,) * len(outs),
        scratch_shapes=list(scratch.values()),
        compiler_params=params(collective_id=1, has_side_effects=True),
        name="block",
    )(*args)


def finish_kernel(*refs):
    ins, outs, bufs, (wide_buf, got, put) = refs[:6], refs[6:13], refs[13:19], refs[19:]
    new, anew, gin, wa, wb, wd = bufs
    takes = [pltpu.make_async_copy(ins[i], bufs[i], got.at[i]) for i in range(6)]
    order = (3, 2, 0, 4, 5, 1)
    for i in order:
        takes[i].start()
    bil_wide = outs[4].shape[1]
    gives = {
        3: [(wide_buf, outs[6])],
        2: [(gin, outs[2])],
        0: [(new, outs[0])],
        4: [(wb.at[:, 0:bil_wide], outs[4]), (wb.at[:, bil_wide:], outs[5])],
        5: [(wd, outs[3])],
        1: [(anew, outs[1])],
    }
    started = []
    for i in order:
        takes[i].wait()
        if i == 3:
            wide_buf[...] = wa[...].astype(F32)
        for src, dst in gives[i]:
            one = pltpu.make_async_copy(src, dst, put.at[len(started)])
            one.start()
            started.append(one)
    for one in started:
        one.wait()


def finish(new, anew, gin, wa, wb, wd):
    shape = jax.ShapeDtypeStruct
    wide = wa.shape[1]
    width = wb.shape[0]
    ins = (new, anew, gin, wa, wb, wd)
    return pl.pallas_call(
        finish_kernel,
        out_shape=(
            shape(new.shape, BF16),
            shape(anew.shape, BF16),
            shape(gin.shape, F32),
            shape(wd.shape, F32),
            shape((width, wb.shape[1] - wide), F32),
            shape((width, wide), F32),
            shape(wa.shape, F32),
        ),
        in_specs=[ANY] * 6,
        out_specs=(ANY,) * 7,
        scratch_shapes=[pltpu.VMEM(one.shape, one.dtype) for one in ins]
        + [pltpu.VMEM(wa.shape, F32), pltpu.SemaphoreType.DMA((6,)), pltpu.SemaphoreType.DMA((7,))],
        compiler_params=params(),
        name="finish",
    )(*ins)


def body(
    groups,
    members,
    edge_emb,
    atom_emb,
    edge_target,
    trip_in,
    trip_out,
    trip_count,
    trip_basis,
    grad_edge,
    grad_atom,
    w_down,
    w_bil,
    w_up,
    w_atom,
):
    scale = 1.0 / math.sqrt(groups * members * edge_emb.shape[1])
    values = dict(
        incoming=trip_in,
        emb=edge_emb[0],
        wdt=w_down.T,
        wbt=w_bil.T,
        wup=w_up,
        target=edge_target,
        atom=atom_emb[0],
        gatom=grad_atom[0],
        count=trip_count,
        outgoing=trip_out,
        basis=trip_basis[0],
        watom=w_atom,
        gedge=grad_edge[0],
    )
    edge_new, atom_new, grad_in, down, bil, up, atom = finish(*block_of(values, members, groups, scale))
    return (edge_new[None], atom_new[None], grad_in[None], down.T, bil.T, up, atom)


def solution(mesh):
    graph = P("dp", "graph")
    rows = P("dp", "graph", None)
    return jax.shard_map(
        functools.partial(body, mesh.shape["dp"], mesh.shape["graph"]),
        mesh=mesh,
        in_specs=(rows, rows, graph, graph, graph, graph, P("dp", None, "graph"), rows, rows)
        + (P(),) * 4,
        out_specs=(rows, rows, rows) + (P(),) * 4,
        check_vma=False,
    )
```

```python
import functools
import math

import jax
import jax.numpy as jnp
from jax import lax
from jax.experimental import pallas as pl
from jax.experimental.pallas import tpu as pltpu
from jax.sharding import PartitionSpec as P

MESH = pl.DeviceIdType.MESH
F32 = jnp.float32
HALVES = 2
TURNS = 4
BF16 = jnp.bfloat16
ATOM_SCALE = 0.25
CAP = 128
LANES = 128
NEAR_FORWARD = 2
NEAR_BACKWARD = 4
SPLIT = 4
BLOCK_NAMES = 4096
BLOCK_FORWARD = 4096
BLOCK_BACKWARD = 2048
ANY = pl.BlockSpec(memory_space=pl.ANY)
VMEM = pl.BlockSpec(memory_space=pltpu.VMEM)
NN = (((1,), (0,)), ((), ()))
NT = (((1,), (1,)), ((), ()))
TN = (((0,), (0,)), ((), ()))


def dot(a, b, dims=NN):
    return lax.dot_general(a, b, dims, preferred_element_type=F32)


def rows_of(shape):
    return lax.broadcasted_iota(jnp.int32, shape, 0)


def hot(index, size):
    return (rows_of((size, index.shape[1])) == index).astype(F32).astype(BF16)


def silu_slope(value):
    logistic = jax.nn.sigmoid(value)
    return logistic * (1.0 + value * (1.0 - logistic))


def silu(value):
    return value * jax.nn.sigmoid(value)


def params(**kw):
    return pltpu.CompilerParams(vmem_limit_bytes=60 * 1024 * 1024, **kw)


def send_to(src, dst, send, recv, **where):
    return pltpu.make_async_remote_copy(
        src_ref=src,
        dst_ref=dst,
        send_sem=send,
        recv_sem=recv,
        device_id=where,
        device_id_type=MESH,
    )


def drain(ref, sem):
    pltpu.make_async_copy(ref, ref, sem).wait()


def each(first, last, act, unroll=False):
    if unroll:
        for k in range(first, last):
            act(k)
        return

    def one(k, c):
        act(k)
        return c

    lax.fori_loop(first, last, one, 0)


def wrap(value, size):
    return jnp.where(value >= size, value - size, value)


def some_rows(ref, index, rows):
    return ref.at[pl.ds(pl.multiple_of(index * rows, rows), rows), :]


def tile_of(ref, row, rows, lane, lanes):
    return ref.at[
        pl.ds(pl.multiple_of(row * rows, rows), rows),
        pl.ds(pl.multiple_of(lane * lanes, lanes), lanes),
    ]


def hot_of_ranks(rank_ref, hot_ref, first, last):
    per = rank_ref.shape[1]
    place = lax.broadcasted_iota(jnp.int32, (CAP, LANES), 0).astype(F32)

    def one(d):
        ranks = rank_ref[d]
        at = pl.ds(pl.multiple_of(d * CAP, CAP), CAP)
        for q in range(per):
            hot_ref[at, q * LANES : (q + 1) * LANES] = (
                (place == ranks[q : q + 1, :]).astype(F32).astype(BF16)
            )

    each(first, last, one)


def block_kernel(members, groups, scale, names_of, *refs):
    r = dict(zip(names_of, refs))
    (in_ref, emb_ref, wdt_ref, wbt_ref, wup_ref, target_ref, atom_ref, gatom_ref, count_ref) = (
        r["incoming"], r["emb"], r["wdt"], r["wbt"], r["wup"], r["target"], r["atom"], r["gatom"], r["count"]
    )
    me = lax.axis_index("graph")
    group = lax.axis_index("dp")
    chips = members // 2
    chip = lax.div(me, 2)
    core = lax.rem(me, 2)
    other = 1 - core
    partner = 2 * chip + other
    all_send, all_recv, many_recv, dp_send, dp_recv, load = (
        r["all_send"], r["all_recv"], r["many_recv"], r["dp_send"], r["dp_recv"], r["load"]
    )

    def peer_at(k):
        return wrap(me + k, members)

    def chip_at(k):
        return wrap(chip + k, chips)

    def chip_from(k):
        return wrap(chip + chips - k, chips)

    def group_at(k):
        return wrap(group + k, groups)

    def mine(c):
        return core * chips + c

    loads = [
        pltpu.make_async_copy(r[name + "_hbm"], r[name], load.at[i])
        for i, name in enumerate(("outgoing", "basis", "watom", "gedge"))
    ]
    for one in loads:
        one.start()
    barrier = pltpu.get_barrier_semaphore()
    each(
        1,
        members,
        lambda k: pl.semaphore_signal(
            barrier, inc=1, device_id={"graph": peer_at(k)}, device_id_type=MESH
        ),
        True,
    )
    each(
        1,
        groups,
        lambda k: pl.semaphore_signal(
            barrier, inc=1, device_id={"dp": group_at(k)}, device_id_type=MESH
        ),
        True,
    )

    table, found, rank_buf, wanted, hots, chosen, name, features = (
        r["table"], r["found"], r["rank_buf"], r["wanted"], r["hots"], r["chosen"], r["name"], r["features"]
    )
    highs = table.shape[0]
    per = highs // members
    width = wdt_ref.shape[0]
    edges, wide = emb_ref.shape
    slots = in_ref.shape[1]
    nblock = math.gcd(slots, BLOCK_NAMES)

    def window(i, block):
        return pl.ds(pl.multiple_of(i * block, block), block)

    def parts_of(i):
        index = in_ref[:, window(i, nblock)]
        return lax.shift_right_logical(index, 7), lax.bitwise_and(index, LANES - 1)

    found[...] = jnp.zeros_like(found)

    def find(i):
        high, low = parts_of(i)
        found[...] += dot(hot(high, highs), hot(low, LANES), NT)

    each(0, slots // nblock, find)
    there = jnp.where(found[...] > 0.0, 1.0, 0.0)
    there16 = there.astype(BF16)
    row = lax.broadcasted_iota(jnp.int32, (LANES, LANES), 0)
    col = lax.broadcasted_iota(jnp.int32, (LANES, LANES), 1)
    upper = (row <= col).astype(F32).astype(BF16)
    hrow = lax.broadcasted_iota(jnp.int32, (highs, highs), 0)
    hcol = lax.broadcasted_iota(jnp.int32, (highs, highs), 1)
    before = ((hcol < hrow) & (lax.div(hcol, per) == lax.div(hrow, per))).astype(F32).astype(BF16)
    ahead = dot(before, there16).astype(BF16)
    ones = jnp.ones((LANES, LANES), BF16)
    rank = dot(there16, upper) + dot(ahead, ones) - 1.0
    rank = jnp.where(there > 0.0, rank, -1.0)
    table[...] = rank.astype(BF16)
    for s in range(members):
        rank_buf[s] = rank[s * per : (s + 1) * per, :]
    proj = dot(wdt_ref[...], emb_ref[...], NT)
    feat = silu(proj).astype(BF16)
    r["down_slope"][...] = silu_slope(proj)
    pl.semaphore_wait(barrier, members - 1 + groups - 1)

    def rank_copy(k):
        peer = peer_at(k)
        return send_to(
            rank_buf.at[peer], wanted.at[members - k], all_send.at[0], all_recv.at[0], graph=peer
        )

    each(1, members, lambda k: rank_copy(k).start(), True)
    wanted[0] = rank_buf[me]

    def look(i):
        high, low = parts_of(i)
        ranks = dot(table[...], hot(high, highs), TN)
        picked = jnp.where(rows_of(ranks.shape) == low, ranks, 0.0)
        rank = jnp.sum(picked, axis=0, keepdims=True).astype(jnp.int32)
        name[:, window(i, nblock)] = lax.div(high, per) * CAP + rank

    looks = slots // nblock
    each(0, looks // 2, look)
    drain(wanted.at[0 : members - 1], all_recv.at[0])

    def feature_tile(index):
        return tile_of(
            features, lax.div(index, NEAR_FORWARD), width, lax.rem(index, NEAR_FORWARD), CAP
        )

    def feature_copy(k):
        return send_to(
            chosen.at[:, k * CAP : (k + 1) * CAP],
            feature_tile(me),
            all_send.at[1],
            all_recv.at[1],
            graph=peer_at(k),
        )

    some = members // TURNS
    for turn in range(TURNS):
        hot_of_ranks(wanted, hots, turn * some, (turn + 1) * some)
        lines = slice(turn * some * CAP, (turn + 1) * some * CAP)
        chosen[:, lines] = dot(feat, hots[lines, :], NT).astype(BF16)
        each(max(turn * some, 1), (turn + 1) * some, lambda k: feature_copy(k).start(), True)
    feature_tile(me)[...] = chosen[:, 0:CAP]
    each(looks // 2, looks, look)
    r["wbil"][...] = wbt_ref[...].astype(F32).T.astype(BF16)
    target = target_ref[...]
    atom_dev = atom_ref.shape[0]
    holder = lax.shift_right_logical(target, atom_dev.bit_length() - 1)
    line = lax.bitwise_and(holder, 1) * chips + lax.shift_right_logical(holder, 1)
    line = line * atom_dev + lax.bitwise_and(target, atom_dev - 1)
    line_hot, line_turn = r["line_hot"], r["line_turn"]
    lined = (rows_of((line_hot.shape[0], edges)) == line).astype(F32)
    line_hot[...] = lined.astype(BF16)
    line_turn[...] = lined.T.astype(BF16)
    drain(chosen.at[:, 0 : (members - 1) * CAP], all_recv.at[1])
    loads[0].wait()
    loads[1].wait()

    outgoing, basis_ref, total_ref = r["outgoing"], r["basis"], r["total"]
    spread = r["spread"]
    fblock = math.gcd(slots, BLOCK_FORWARD)
    far_shift = (NEAR_FORWARD * CAP).bit_length() - 1
    far = members // NEAR_FORWARD
    total_ref[...] = jnp.zeros_like(total_ref)

    def place_of(i, block):
        at = i * block + lax.broadcasted_iota(jnp.int32, (1, block), 1)
        return jnp.where(at < count_ref[0, 0], outgoing[:, window(i, block)], -1)

    def forward(i):
        here = window(i, fblock)
        index = name[:, here]
        group_of = lax.shift_right_logical(index, far_shift)
        all_wide = dot(features[...], hot(lax.bitwise_and(index, NEAR_FORWARD * CAP - 1), NEAR_FORWARD * CAP))
        feat = all_wide[0:width]
        for k in range(1, far):
            feat = jnp.where(group_of == k, all_wide[k * width : (k + 1) * width], feat)
        basis = basis_ref[:, here].astype(F32)
        for b in range(basis.shape[0]):
            spread[b * width : (b + 1) * width, :] = (basis[b : b + 1, :] * feat).astype(BF16)
        total_ref[...] += dot(spread[...], hot(place_of(i, fblock), edges), NT)

    each(0, slots // fblock, forward)

    parts, half, pair, arrived, grads, slope, gnew = (
        r["parts"], r["half"], r["pair"], r["arrived"], r["grads"], r["slope"], r["gnew"]
    )
    new_ref, anew_ref = r["new"], r["anew"]

    def leave(i):
        key = ("new", "anew", "gin", "wa_all", "wb_all", "wd_all")[i]
        return pltpu.make_async_copy(r[key], r[key + "_hbm"], load.at[4 + i])

    total = total_ref[...]
    high = total.astype(BF16)
    low = (total - high.astype(F32)).astype(BF16)
    gathered32 = dot(wbt_ref[...], high) + dot(wbt_ref[...], low)
    gathered = gathered32.astype(BF16)
    gathered_rows = gathered32.T.astype(BF16)
    part = wide // HALVES

    def pair_copy(q):
        rows = parts.shape[0] // 2
        lanes = slice(q * part, (q + 1) * part)
        return send_to(
            parts.at[pl.ds(pl.multiple_of(other * rows, rows), rows), lanes],
            half.at[:, lanes],
            all_send.at[2],
            many_recv.at[0, q],
            graph=partner,
        )

    for q in range(HALVES):
        lanes = slice(q * part, (q + 1) * part)
        update = dot(gathered_rows, wup_ref[:, lanes])
        new = (emb_ref[:, lanes].astype(F32) + silu(update)).astype(BF16)
        new_ref[:, lanes] = new
        slope[:, lanes] = update
        parts[:, lanes] = dot(line_hot[...], new).astype(BF16)
        pair_copy(q).start()

    def chip_copy(k, lanes):
        c = chip_at(k)
        return send_to(
            some_rows(pair, c, atom_dev).at[:, lanes],
            arrived.at[chip, :, lanes],
            all_send.at[3],
            all_recv.at[3],
            graph=2 * c + core,
        )

    for q in range(HALVES):
        lanes = slice(q * part, (q + 1) * part)
        rows = parts.shape[0] // 2
        own = parts[pl.ds(pl.multiple_of(core * rows, rows), rows), lanes].astype(F32)
        pair_copy(q).wait_recv()
        pair[:, lanes] = (own + half[:, lanes].astype(F32)).astype(BF16)
        each(1, chips, lambda k: chip_copy(k, lanes).start(), True)
    arrived[chip] = some_rows(pair, chip, atom_dev)[...]
    slope[...] = silu_slope(slope[...])
    loads[2].wait()
    loads[3].wait()
    watom_ref, gedge_ref = r["watom"], r["gedge"]
    drain(arrived.at[0 : chips - 1], all_recv.at[3])

    asum = jnp.sum(arrived[...].astype(F32), axis=0).astype(BF16)
    pre = ATOM_SCALE * dot(asum, watom_ref[...])
    grad_pre = (gatom_ref[...].astype(F32) * silu_slope(pre)).astype(BF16)
    some_rows(grads, mine(chip), atom_dev)[...] = (
        ATOM_SCALE * dot(grad_pre, watom_ref[...], NT)
    ).astype(BF16)

    def grad_copy(k):
        rows = some_rows(grads, mine(chip), atom_dev)
        return send_to(rows, rows, all_send.at[4], many_recv.at[1, k], graph=2 * chip_at(k) + core)

    def grad_pass(k):
        rows = some_rows(grads, mine(chip_from(k)), atom_dev)
        return send_to(rows, rows, all_send.at[5], all_recv.at[5], graph=partner)

    def grad_forward(k):
        grad_copy(k).wait_recv()
        grad_pass(k).start()

    each(1, chips, lambda k: grad_copy(k).start(), True)
    grad_pass(0).start()
    wa, wb = r["wa"], r["wb"]
    anew_ref[...] = (atom_ref[...].astype(F32) + silu(pre)).astype(BF16)
    wa[...] = (ATOM_SCALE * dot(asum, grad_pre, TN)).astype(BF16)
    def wa_duo():
        return send_to(
            some_rows(wa, other, wa.shape[0] // 2), r["wa_half"], all_send.at[6], all_recv.at[6], graph=partner
        )

    leave(0).start()
    leave(1).start()
    each(1, chips, grad_forward, True)
    wa_duo().start()
    drain(half, all_recv.at[5])

    picked = dot(line_turn[...], grads[...])
    grad_new = gedge_ref[...].astype(F32) + picked
    gnew[...] = grad_new
    grad_update = (grad_new * slope[...]).astype(BF16)
    bil_wide = wbt_ref.shape[1]
    wb[:, bil_wide:] = dot(gathered, grad_update)
    gg = dot(wup_ref[...], grad_update, NT).astype(BF16)
    wb[:, :bil_wide] = dot(gg, total_ref[...].astype(BF16), NT)

    wa_half, wa_pair, wa_in, wa_dp, wa_all = r["wa_half"], r["wa_pair"], r["wa_in"], r["wa_dp"], r["wa_all"]
    wb_half, wb_pair, wb_in, wb_dp, wb_all = r["wb_half"], r["wb_pair"], r["wb_in"], r["wb_dp"], r["wb_all"]
    wa_rows = wa.shape[0] // members
    wb_rows = wb.shape[0] // 8
    wb_lanes = wb.shape[1] // SPLIT
    wb_split = chips // SPLIT

    def wb_tile(ref, c, base):
        return tile_of(ref, base * wb_split + lax.div(c, SPLIT), wb_rows, lax.rem(c, SPLIT), wb_lanes)

    def wb_duo():
        return send_to(
            some_rows(wb, other, wb.shape[0] // 2), wb_half, all_send.at[7], all_recv.at[7], graph=partner
        )

    def wa_far(k):
        c = chip_at(k)
        return send_to(
            some_rows(wa_pair, c, wa_rows), wa_in.at[chip], all_send.at[8], all_recv.at[8], graph=2 * c + core
        )

    def wb_far(k):
        c = chip_at(k)
        return send_to(
            wb_tile(wb_pair, c, 0), wb_in.at[chip], all_send.at[9], all_recv.at[9], graph=2 * c + core
        )

    def wa_group(k):
        return send_to(wa_dp.at[group], wa_dp.at[group], dp_send.at[0], dp_recv.at[0], dp=group_at(k))

    def wb_group(k):
        return send_to(wb_dp.at[group], wb_dp.at[group], dp_send.at[1], dp_recv.at[1], dp=group_at(k))

    def wa_back(k):
        rows = some_rows(wa_all, mine(chip), wa_rows)
        return send_to(rows, rows, all_send.at[10], all_recv.at[10], graph=2 * chip_at(k) + core)

    def wb_back(k):
        tile = wb_tile(wb_all, chip, core)
        return send_to(tile, tile, all_send.at[11], all_recv.at[11], graph=2 * chip_at(k) + core)

    def wa_pass():
        rows = some_rows(wa_all, core, wa.shape[0] // 2)
        return send_to(rows, rows, all_send.at[12], all_recv.at[12], graph=partner)

    def wb_pass():
        rows = some_rows(wb_all, core, wb.shape[0] // 2)
        return send_to(rows, rows, all_send.at[13], all_recv.at[13], graph=partner)

    def sums_pair():
        wa_duo().wait_recv()
        wb_duo().wait_recv()
        wa_pair[...] = (
            some_rows(wa, core, wa.shape[0] // 2)[...].astype(F32) + wa_half[...].astype(F32)
        ).astype(BF16)
        wb_pair[...] = some_rows(wb, core, wb.shape[0] // 2)[...] + wb_half[...]

    def sums_far():
        def go(k):
            wa_far(k).start()
            wb_far(k).start()

        each(1, chips, go, True)
        wa_in[chip] = some_rows(wa_pair, chip, wa_rows)[...]
        wb_in[chip] = wb_tile(wb_pair, chip, 0)[...]

    def sums_group():
        drain(wa_in.at[0 : chips - 1], all_recv.at[8])
        drain(wb_in.at[0 : chips - 1], all_recv.at[9])
        wa_dp[group] = jnp.sum(wa_in[...].astype(F32), axis=0)
        wb_dp[group] = jnp.sum(wb_in[...], axis=0)

        def go(k):
            wa_group(k).start()
            wb_group(k).start()

        each(1, groups, go, True)

    def sums_back():
        drain(wa_dp.at[0 : groups - 1], dp_recv.at[0])
        drain(wb_dp.at[0 : groups - 1], dp_recv.at[1])
        some_rows(wa_all, mine(chip), wa_rows)[...] = (scale * jnp.sum(wa_dp[...], axis=0)).astype(BF16)
        wb_tile(wb_all, chip, core)[...] = scale * jnp.sum(wb_dp[...], axis=0)

        def go(k):
            wa_back(k).start()
            wb_back(k).start()

        each(1, chips, go, True)

    def sums_pass():
        drain(wa_in.at[0 : chips - 1], all_recv.at[10])
        drain(wb_in.at[0 : chips - 1], all_recv.at[11])
        wa_pass().start()
        wb_pass().start()

    wb_duo().start()
    gg_two = r["gg_two"]
    gg_two[0:width, :] = gg[:, 0 : edges // 2]
    gg_two[width:, :] = gg[:, edges // 2 :]

    sent, back = r["sent"], r["back"]
    named, wbil = r["named"], r["wbil"]
    block = math.gcd(slots, BLOCK_BACKWARD)
    blocks = slots // block
    back_far = members // NEAR_BACKWARD
    back_shift = (NEAR_BACKWARD * CAP).bit_length() - 1
    named[...] = jnp.zeros_like(named)
    acts = {1: sums_pair, 2: sums_far, 9: sums_group, 11: sums_back}
    masked = r["masked"]

    def backward(i):
        for at, act in acts.items():
            pl.when(i == at * blocks // 16)(act)
        here = window(i, block)
        place = place_of(i, block)
        both = dot(gg_two[...], hot(lax.bitwise_and(place, edges // 2 - 1), edges // 2))
        first = lax.shift_right_arithmetic(place, edges.bit_length() - 2)
        taken = jnp.where(first == 0, both[0:width], jnp.where(first == 1, both[width:], 0.0)).astype(BF16)
        backed = dot(wbil[...], taken)
        basis = basis_ref[:, here].astype(F32)
        grad = basis[0:1, :] * backed[0:width]
        for b in range(1, basis.shape[0]):
            grad = grad + basis[b : b + 1, :] * backed[b * width : (b + 1) * width]
        source = lax.shift_right_logical(name[:, here], back_shift)
        for k in range(back_far):
            masked[k * width : (k + 1) * width, :] = jnp.where(source == k, grad, 0.0).astype(BF16)
        near = lax.bitwise_and(name[:, window(i, block)], NEAR_BACKWARD * CAP - 1)
        named[...] += dot(masked[...], hot(near, NEAR_BACKWARD * CAP), NT)

    each(0, blocks, backward)

    sent[...] = named[...].astype(BF16)

    def sent_tile(index):
        return tile_of(sent, lax.div(index, NEAR_BACKWARD), width, lax.rem(index, NEAR_BACKWARD), CAP)

    def back_copy(k):
        peer = peer_at(k)
        there = members - k
        return send_to(
            sent_tile(peer),
            back.at[:, there * CAP : (there + 1) * CAP],
            all_send.at[14],
            all_recv.at[14],
            graph=peer,
        )

    each(1, members, lambda k: back_copy(k).start(), True)
    back[:, 0:CAP] = sent_tile(me)[...]
    sums_pass()
    wa_pass().wait_recv()
    wb_pass().wait_recv()
    leave(3).start()
    leave(4).start()
    drain(back.at[:, 0 : (members - 1) * CAP], all_recv.at[14])
    grad = dot(back[...], hots[...])
    grad = (grad * r["down_slope"][...]).astype(BF16)

    wd, wd_in, wd_dp, wd_all = r["wd"], r["wd_in"], r["wd_dp"], r["wd_all"]
    wd[...] = dot(grad, emb_ref[...])

    def wd_tile(ref, index):
        return tile_of(ref, lax.div(index, SPLIT), ref.shape[0] * SPLIT // members, lax.rem(index, SPLIT), LANES)

    def wd_far(k):
        peer = peer_at(k)
        return send_to(wd_tile(wd, peer), wd_in.at[me], all_send.at[15], all_recv.at[15], graph=peer)

    def wd_group(k):
        return send_to(wd_dp.at[group], wd_dp.at[group], dp_send.at[2], dp_recv.at[2], dp=group_at(k))

    def wd_back(k):
        tile = wd_tile(wd_all, me)
        return send_to(tile, tile, all_send.at[16], all_recv.at[16], graph=peer_at(k))

    each(1, members, lambda k: wd_far(k).start(), True)
    wd_in[me] = wd_tile(wd, me)[...]
    r["gin"][...] = gnew[...] + dot(grad, wdt_ref[...], TN)
    leave(2).start()
    drain(wd_in.at[0 : members - 1], all_recv.at[15])
    wd_dp[group] = jnp.sum(wd_in[...], axis=0)
    each(1, groups, lambda k: wd_group(k).start(), True)
    drain(wd_dp.at[0 : groups - 1], dp_recv.at[2])
    wd_tile(wd_all, me)[...] = scale * jnp.sum(wd_dp[...], axis=0)
    each(1, members, lambda k: wd_back(k).start(), True)

    drain(wanted.at[0 : members - 1], all_send.at[0])
    drain(chosen.at[:, 0 : (members - 1) * CAP], all_send.at[1])
    drain(half, all_send.at[2])
    drain(arrived.at[0 : chips - 1], all_send.at[3])
    drain(arrived.at[0 : chips - 1], all_send.at[4])
    drain(half, all_send.at[5])
    wa_duo().wait_send()
    wb_duo().wait_send()
    drain(wa_in.at[0 : chips - 1], all_send.at[8])
    drain(wb_in.at[0 : chips - 1], all_send.at[9])
    drain(wa_in.at[0 : chips - 1], all_send.at[10])
    drain(wb_in.at[0 : chips - 1], all_send.at[11])
    wa_pass().wait_send()
    wb_pass().wait_send()
    drain(wa_dp.at[0 : groups - 1], dp_send.at[0])
    drain(wb_dp.at[0 : groups - 1], dp_send.at[1])
    drain(wd_dp.at[0 : groups - 1], dp_send.at[2])
    drain(back.at[:, 0 : (members - 1) * CAP], all_send.at[14])
    drain(wd_in.at[0 : members - 1], all_send.at[15])
    drain(wd_in.at[0 : members - 1], all_send.at[16])
    drain(wd_in.at[0 : members - 1], all_recv.at[16])
    leave(5).start()
    for i in range(6):
        leave(i).wait()


def block_of(values, members, groups, scale):
    shape = jax.ShapeDtypeStruct
    edges, wide = values["emb"].shape
    atom_dev = values["atom"].shape[0]
    atoms = atom_dev * members
    width = values["wdt"].shape[0]
    slots = values["incoming"].shape[1]
    rows = values["wbt"].shape[1]
    chips = members // 2
    highs = members * edges // LANES
    per = highs // members
    all_wide = rows + wide
    piece = (width // 8, all_wide // SPLIT)
    wa_piece = (wide // members, wide)
    wd_piece = (width * SPLIT // members, wide // SPLIT)
    far = members // NEAR_FORWARD
    back_far = members // NEAR_BACKWARD
    late = ("outgoing", "basis", "watom", "gedge")
    ins, specs, args = [], [], []
    for key, value in values.items():
        if key in late:
            ins.append(key + "_hbm")
            specs.append(ANY)
        else:
            ins.append(key)
            specs.append(pl.BlockSpec(memory_space=pltpu.SMEM) if key == "count" else VMEM)
        args.append(value)
    outs = {
        "new": shape((edges, wide), BF16),
        "anew": shape((atom_dev, wide), BF16),
        "gin": shape((edges, wide), F32),
        "wa_all": shape((wide, wide), BF16),
        "wb_all": shape((width, all_wide), F32),
        "wd_all": shape((width, wide), F32),
    }
    scratch = {key: pltpu.VMEM(values[key].shape, values[key].dtype) for key in late}
    scratch |= {key: pltpu.VMEM(out.shape, out.dtype) for key, out in outs.items()}
    scratch |= {
        "table": pltpu.VMEM((highs, LANES), BF16),
        "found": pltpu.VMEM((highs, LANES), F32),
        "rank_buf": pltpu.VMEM((members, per, LANES), F32),
        "wanted": pltpu.VMEM((members, per, LANES), F32),
        "hots": pltpu.VMEM((members * CAP, edges), BF16),
        "chosen": pltpu.VMEM((width, members * CAP), BF16),
        "name": pltpu.VMEM((1, slots), jnp.int32),
        "features": pltpu.VMEM((far * width, NEAR_FORWARD * CAP), BF16),
        "down_slope": pltpu.VMEM((width, edges), F32),
        "wbil": pltpu.VMEM((rows, width), BF16),
        "spread": pltpu.VMEM((rows, math.gcd(slots, BLOCK_FORWARD)), BF16),
        "total": pltpu.VMEM((rows, edges), F32),
        "line_hot": pltpu.VMEM((atoms, edges), BF16),
        "line_turn": pltpu.VMEM((edges, atoms), BF16),
        "parts": pltpu.VMEM((atoms, wide), BF16),
        "half": pltpu.VMEM((atoms // 2, wide), BF16),
        "pair": pltpu.VMEM((atoms // 2, wide), BF16),
        "arrived": pltpu.VMEM((chips, atom_dev, wide), BF16),
        "grads": pltpu.VMEM((atoms, wide), BF16),
        "slope": pltpu.VMEM((edges, wide), F32),
        "gnew": pltpu.VMEM((edges, wide), F32),
        "wa": pltpu.VMEM((wide, wide), BF16),
        "wa_half": pltpu.VMEM((wide // 2, wide), BF16),
        "wa_pair": pltpu.VMEM((wide // 2, wide), BF16),
        "wa_in": pltpu.VMEM((chips, *wa_piece), BF16),
        "wa_dp": pltpu.VMEM((groups, *wa_piece), F32),
        "wb": pltpu.VMEM((width, all_wide), F32),
        "wb_half": pltpu.VMEM((width // 2, all_wide), F32),
        "wb_pair": pltpu.VMEM((width // 2, all_wide), F32),
        "wb_in": pltpu.VMEM((chips, *piece), F32),
        "wb_dp": pltpu.VMEM((groups, *piece), F32),
        "gg_two": pltpu.VMEM((2 * width, edges // 2), BF16),
        "named": pltpu.VMEM((back_far * width, NEAR_BACKWARD * CAP), F32),
        "masked": pltpu.VMEM((back_far * width, math.gcd(slots, BLOCK_BACKWARD)), BF16),
        "sent": pltpu.VMEM((back_far * width, NEAR_BACKWARD * CAP), BF16),
        "back": pltpu.VMEM((width, members * CAP), BF16),
        "wd": pltpu.VMEM((width, wide), F32),
        "wd_in": pltpu.VMEM((members, *wd_piece), F32),
        "wd_dp": pltpu.VMEM((groups, *wd_piece), F32),
        "all_send": pltpu.SemaphoreType.DMA((17,)),
        "all_recv": pltpu.SemaphoreType.DMA((17,)),
        "many_recv": pltpu.SemaphoreType.DMA((2, chips)),
        "dp_send": pltpu.SemaphoreType.DMA((3,)),
        "dp_recv": pltpu.SemaphoreType.DMA((3,)),
        "load": pltpu.SemaphoreType.DMA((10,)),
    }
    return pl.pallas_call(
        functools.partial(block_kernel, members, groups, scale, (*ins, *(key + "_hbm" for key in outs), *scratch)),
        out_shape=tuple(outs.values()),
        in_specs=specs,
        out_specs=(ANY,) * len(outs),
        scratch_shapes=list(scratch.values()),
        compiler_params=params(collective_id=1, has_side_effects=True),
        name="block",
    )(*args)


def finish_kernel(*refs):
    ins, outs, bufs, (wide_buf, got, put) = refs[:6], refs[6:13], refs[13:19], refs[19:]
    new, anew, gin, wa, wb, wd = bufs
    takes = [pltpu.make_async_copy(ins[i], bufs[i], got.at[i]) for i in range(6)]
    order = (3, 2, 0, 4, 5, 1)
    for i in order:
        takes[i].start()
    bil_wide = outs[4].shape[1]
    gives = {
        3: [(wide_buf, outs[6])],
        2: [(gin, outs[2])],
        0: [(new, outs[0])],
        4: [(wb.at[:, 0:bil_wide], outs[4]), (wb.at[:, bil_wide:], outs[5])],
        5: [(wd, outs[3])],
        1: [(anew, outs[1])],
    }
    started = []
    for i in order:
        takes[i].wait()
        if i == 3:
            wide_buf[...] = wa[...].astype(F32)
        for src, dst in gives[i]:
            one = pltpu.make_async_copy(src, dst, put.at[len(started)])
            one.start()
            started.append(one)
    for one in started:
        one.wait()


def finish(new, anew, gin, wa, wb, wd):
    shape = jax.ShapeDtypeStruct
    wide = wa.shape[1]
    width = wb.shape[0]
    ins = (new, anew, gin, wa, wb, wd)
    return pl.pallas_call(
        finish_kernel,
        out_shape=(
            shape(new.shape, BF16),
            shape(anew.shape, BF16),
            shape(gin.shape, F32),
            shape(wd.shape, F32),
            shape((width, wb.shape[1] - wide), F32),
            shape((width, wide), F32),
            shape(wa.shape, F32),
        ),
        in_specs=[ANY] * 6,
        out_specs=(ANY,) * 7,
        scratch_shapes=[pltpu.VMEM(one.shape, one.dtype) for one in ins]
        + [pltpu.VMEM(wa.shape, F32), pltpu.SemaphoreType.DMA((6,)), pltpu.SemaphoreType.DMA((7,))],
        compiler_params=params(),
        name="finish",
    )(*ins)


def body(
    groups,
    members,
    edge_emb,
    atom_emb,
    edge_target,
    trip_in,
    trip_out,
    trip_count,
    trip_basis,
    grad_edge,
    grad_atom,
    w_down,
    w_bil,
    w_up,
    w_atom,
):
    scale = 1.0 / math.sqrt(groups * members * edge_emb.shape[1])
    values = dict(
        incoming=trip_in,
        emb=edge_emb[0],
        wdt=w_down.T,
        wbt=w_bil.T,
        wup=w_up,
        target=edge_target,
        atom=atom_emb[0],
        gatom=grad_atom[0],
        count=trip_count,
        outgoing=trip_out,
        basis=trip_basis[0],
        watom=w_atom,
        gedge=grad_edge[0],
    )
    edge_new, atom_new, grad_in, down, bil, up, atom = finish(*block_of(values, members, groups, scale))
    return (edge_new[None], atom_new[None], grad_in[None], down.T, bil.T, up, atom)


def solution(mesh):
    graph = P("dp", "graph")
    rows = P("dp", "graph", None)
    return jax.shard_map(
        functools.partial(body, mesh.shape["dp"], mesh.shape["graph"]),
        mesh=mesh,
        in_specs=(rows, rows, graph, graph, graph, graph, P("dp", None, "graph"), rows, rows)
        + (P(),) * 4,
        out_specs=(rows, rows, rows) + (P(),) * 4,
        check_vma=False,
    )
```
